32 devices in a mesh: row: 4 (over y, core), col: 8 (over z, x).
Axes of the slice: x: 2, y: 2, z: 4, core: 2. Of those that a mesh axis runs over, the one named last changes fastest.
Arguments:
- resid_deriv: bfloat16 [256, 512, 1024], P(('row', 'col')), may hold values from -0.03125 to 0.03125
- local_deriv: bfloat16 [256, 512, 128], P(('row', 'col'))
- inv_factor: float32 [256, 128, 128], P(('row', 'col'))
- block_ids: int32 [256, 8], P(('row', 'col')), may hold values from 0 to 31, as said below
- right_sides: float32 [4096, 256], P(('col', 'row')), may hold values from -6 to 6
- damping: float32 [4096], P(('col', 'row')), may hold values from 0.25 to 2
Outputs:
- normal: float32 [8, 4, 128, 4096], P(None, 'row', None, 'col')
- solution: float32 [4096, 256], P(('col', 'row'))
The draws below stay inside these ranges and needn't reach their ends.
Inputs may be any that keep to these rules, and one draw needn't show every extreme that they name: `block_ids`: all 8 bundles in each aligned block of 8 rows name the same 8 distinct blocks, each bundle in its own order. Among one such set, the values block // 4 are distinct and every residue block % 4 appears exactly 2 times.
All inputs are finite; a program needn't handle non-finite values.
Results may differ from the reference program's by a relative error of at most 0.00038.
Values sent between devices are 32-bit elements; how exact they have to be, the bound alone decides.
No kernel may reach another device: no remote copies, remote signals or barrier semaphores. Data moves between devices by JAX's collectives and lax.ppermute only.
A program may use at most 128 MiB of HBM per device.

```python
import math
import jax
import jax.numpy as jnp
from jax import lax

PB = 128
GP = 1024
NL = 128
M = 512
BPD = 8
RHS = 256
ITERS = 3
BK = 8
CT = 4
RT = 8
NG = 4096
BUNDLES = 256
N_ROW = 4


def sector_draw(key):
    devices_all = BUNDLES // BPD
    keys = jax.random.split(jax.random.fold_in(key, 31), 4)
    popular = jax.random.permutation(keys[0], RT).astype(jnp.int32) + 1
    scores = jax.random.randint(keys[1], (devices_all, RT), 0, 65536, dtype=jnp.int32) * popular[None, :]
    scores = scores * RT + jnp.arange(RT, dtype=jnp.int32)[None, :]
    _, groups = lax.top_k(scores, BK)
    shuffle = jax.random.randint(keys[2], (devices_all, BK), 0, 65536, dtype=jnp.int32) * BK
    shuffle = shuffle + jnp.arange(BK, dtype=jnp.int32)[None, :]
    residue = jnp.argsort(shuffle, axis=1).astype(jnp.int32) % CT
    sector = groups.astype(jnp.int32) * CT + residue
    spread = jnp.repeat(sector, BPD, axis=0)
    mixing = jax.random.randint(keys[3], (BUNDLES, BK), 0, 65536, dtype=jnp.int32) * BK
    mixing = mixing + jnp.arange(BK, dtype=jnp.int32)[None, :]
    return jnp.take_along_axis(spread, jnp.argsort(mixing, axis=1), axis=1).astype(jnp.int32)


def local_pair(key):
    base = jax.random.normal(jax.random.fold_in(key, 7), (BUNDLES, M, NL), jnp.float32)
    local_part = base.astype(jnp.bfloat16)
    widened = local_part.astype(jnp.float32)
    inner = jnp.einsum('bmn,bmk->bnk', widened, widened, precision=lax.Precision.HIGHEST)
    lower_part = lax.linalg.cholesky(inner)
    identity = jnp.broadcast_to(jnp.eye(NL, dtype=jnp.float32), inner.shape)
    factor = lax.linalg.triangular_solve(lower_part, identity, left_side=True, lower=True, transpose_a=True)
    return (local_part, factor)


def draw_block_ids(key, part):
    return sector_draw(key)


def draw_local_deriv(key, part):
    local_part, factor = local_pair(key)
    return local_part


def draw_inv_factor(key, part):
    local_part, factor = local_pair(key)
    return factor


def block_levels(own_key, shape, cuts, low, largest):
    def one(position, shards_of):
        draws = jax.random.uniform(jax.random.fold_in(jax.random.fold_in(own_key, 6), position), (shards_of,), jnp.float32, low / len(cuts), largest / len(cuts))
        return jnp.repeat(jnp.exp(draws), shape[position] // shards_of).reshape((-1,) + (1,) * (len(shape) - position - 1))

    level = one(*cuts[0])
    for cut in cuts[1:]:
        level = level * one(*cut)
    return level


def gaussian(stream_key, dims, scale, bound, cuts=(), held_as=jnp.bfloat16):
    gain = block_levels(stream_key, dims, cuts, -0.22, 0.18) if cuts else 1.0
    entries = jax.random.normal(stream_key, dims, jnp.float32) * scale * gain
    return jnp.minimum(jnp.maximum(entries, -bound), bound).astype(held_as)


def setup_inputs(seed: int = 0) -> dict:
    streams_of = jax.random.split(jax.random.key(seed), 7)
    return {
        "resid_deriv": gaussian(streams_of[0], (BUNDLES, M, GP), (BPD * BK * M) ** -0.5, 0.03125, ((0, 32),)),
        "local_deriv": draw_local_deriv(jax.random.fold_in(streams_of[6], 71), 0),
        "inv_factor": draw_inv_factor(jax.random.fold_in(streams_of[6], 71), 0),
        "block_ids": draw_block_ids(jax.random.fold_in(streams_of[6], 71), 0),
        "right_sides": gaussian(streams_of[4], (NG, RHS), 1.0, 6.0, ((0, 32),), jnp.float32),
        "damping": jnp.clip(jnp.exp(math.log(2.0) - 2.0794415 * jax.random.uniform(streams_of[5], (NG,), jnp.float32) ** block_levels(streams_of[5], (NG,), ((0, 32),), -0.2, 0.2)), 0.25, 2.0),
    }


cheb_low = 0.05
cheb_high = 2.0

def reference(resid_deriv, local_deriv, inv_factor, block_ids, right_sides, damping):
    block_count = NG // PB
    offsets = jnp.arange(PB, dtype=jnp.int32)

    def add_bundle(running, inputs):
        derivs, local_part, factor, block_list = inputs
        coupled = jnp.dot(derivs.T.astype(jnp.float32), local_part.astype(jnp.float32), preferred_element_type=jnp.float32)
        projected = jnp.dot(coupled, factor, precision=lax.Precision.HIGHEST).astype(jnp.bfloat16)
        reduced = jnp.dot(derivs.T.astype(jnp.float32), derivs.astype(jnp.float32), preferred_element_type=jnp.float32) - jnp.dot(projected.astype(jnp.float32), projected.T.astype(jnp.float32), preferred_element_type=jnp.float32)
        flat_index = (block_list[:, None].astype(jnp.int32) * PB + offsets[None, :]).reshape(-1).astype(jnp.int32)
        running = running.at[flat_index[:, None], flat_index[None, :]].add(reduced)
        return (running, None)
    matrix, _ = lax.scan(add_bundle, jnp.zeros((NG, NG), jnp.float32), (resid_deriv, local_deriv, inv_factor, block_ids))
    diag_index = jnp.arange(NG, dtype=jnp.int32)
    matrix = matrix.at[diag_index, diag_index].add(damping)

    def take_tile(offset):
        return lax.dynamic_slice(matrix, (offset, offset), (PB, PB))
    starts = jnp.arange(block_count, dtype=jnp.int32) * PB
    pivots = jax.vmap(take_tile)(starts)
    factors = lax.linalg.cholesky(pivots)

    def precondition(vector_in):
        pieces = vector_in.reshape(block_count, PB, vector_in.shape[1])
        forward = lax.linalg.triangular_solve(factors, pieces, left_side=True, lower=True)
        solved = lax.linalg.triangular_solve(factors, forward, left_side=True, lower=True, transpose_a=True)
        return solved.reshape(vector_in.shape)
    center = (cheb_high + cheb_low) / 2.0
    radius = (cheb_high - cheb_low) / 2.0
    ratio = center / radius
    weight_now = 1.0 / ratio
    residual = right_sides
    update = precondition(residual) / center
    solution = jnp.zeros_like(right_sides)
    for sweep in range(ITERS):
        solution = solution + update
        if sweep + 1 < ITERS:
            residual = residual - jnp.dot(matrix, update, precision=lax.Precision.HIGHEST)
            weight_next = 1.0 / (2.0 * ratio - weight_now)
            update = weight_next * weight_now * update + 2.0 * weight_next / radius * precondition(residual)
            weight_now = weight_next
    normal = matrix.reshape(block_count // N_ROW, N_ROW, PB, NG)
    return (normal, solution)
```

```python
import functools

import jax
import jax.numpy as jnp
from jax import lax
from jax.experimental import pallas as pl
from jax.experimental.pallas import tpu as pltpu
from jax.sharding import PartitionSpec as P


PB = 128
ITERS = 3

cheb_low = 0.05
cheb_high = 2.0
center = (cheb_high + cheb_low) / 2.0
radius = (cheb_high - cheb_low) / 2.0
ratio = center / radius

BOTH = ("row", "col")
VMEM = pl.BlockSpec(memory_space=pltpu.VMEM)
SMEM = pl.BlockSpec(memory_space=pltpu.SMEM)
ANY = pl.BlockSpec(memory_space=pl.ANY)
f32_dot = functools.partial(jnp.dot, preferred_element_type=jnp.float32)


def params(mib):
    return pltpu.CompilerParams(vmem_limit_bytes=mib << 20)


def split(x):
    high = x.astype(jnp.bfloat16)
    return high, (x - high.astype(jnp.float32)).astype(jnp.bfloat16)


def dot_split(a, b):
    (ah, al), (bh, bl) = a, b
    return f32_dot(ah, bh) + (f32_dot(ah, bl) + f32_dot(al, bh))


def chunk_list(capacity):
    chunks = [(0, 0, PB)]
    for slot in range(1, capacity):
        chunks += [(slot, 0, PB // 2), (slot, PB // 2, PB // 2)]
    return chunks


def region_kernel(n_row, n_col, chunks, ids, resid, local, factor, *refs):
    outs = refs[: len(chunks)]
    cols, rows, stage, sector, in_sem, out_sem = refs[len(chunks) :]
    bundles, blocks = ids.shape
    m = resid.shape[1]
    depth = bundles * m

    for b in range(bundles):
        for k in range(blocks):
            me = ids[b, k]
            rank = jnp.int32(0)
            for j in range(blocks):
                rank = rank + (ids[b, j] < me).astype(jnp.int32)
            pltpu.make_async_copy(
                resid.at[b, :, pl.ds(k * PB, PB)], cols.at[rank, pl.ds(b * m, m), :], in_sem.at[b]
            ).start()
            if b == 0:
                sector[rank] = me

    for b in range(bundles):
        here = cols.at[:, pl.ds(b * m, m), :]
        pltpu.make_async_copy(here, here, in_sem.at[b]).wait()
        for p in range(blocks):
            rows[p * PB : (p + 1) * PB, b * m : (b + 1) * m] = cols[p, b * m : (b + 1) * m, :].T
        coupled = f32_dot(rows[:, b * m : (b + 1) * m], local[b])
        projected = dot_split(split(coupled), split(factor[b])).astype(jnp.bfloat16)
        n = projected.shape[1]
        at = depth + b * n
        rows[:, at : at + n] = -projected
        for p in range(blocks):
            cols[p, at : at + n, :] = projected[p * PB : (p + 1) * PB].T

    def send(g, h):
        mine, other = sector[g], sector[h]
        residue = lax.rem(mine, n_row)
        rank = jnp.int32(0)
        for j in range(g):
            rank = rank + (lax.rem(sector[j], n_row) == residue).astype(jnp.int32)
        owner = residue * n_col + lax.div(other, n_row)
        if g == h:
            slot = jnp.int32(0)
        elif g < h:
            slot = rank + (lax.rem(other, n_row) == residue).astype(jnp.int32)
        else:
            slot = rank
        for out, (at_slot, first, count) in zip(outs, chunks):

            @pl.when(slot == at_slot)
            def _():
                pltpu.make_async_copy(
                    stage.at[g, h, pl.ds(first, count)], out.at[owner], out_sem
                ).start()

    for i in range(0, blocks, 2):
        for j in range(i, blocks, 2):
            right = jnp.concatenate([cols[j], cols[j + 1]], axis=1)
            total = f32_dot(rows[i * PB : (i + 2) * PB, :], right)
            for x in range(2):
                for y in range(2):
                    tile = total[x * PB : (x + 1) * PB, y * PB : (y + 1) * PB]
                    stage[i + x, j + y] = tile
                    send(i + x, j + y)
                    if i != j:
                        stage[j + y, i + x] = tile.T
                        send(j + y, i + x)
    pltpu.make_async_copy(stage, stage, out_sem).wait()


def region(ids, resid, local, factor, n_row, n_col, chunks):
    bundles, m, gp = resid.shape
    blocks, n = ids.shape[1], local.shape[2]
    depth = bundles * (m + n)
    return pl.pallas_call(
        functools.partial(region_kernel, n_row, n_col, chunks),
        out_shape=[
            jax.ShapeDtypeStruct((n_row * n_col, count, PB), jnp.float32) for _, _, count in chunks
        ],
        in_specs=[SMEM, ANY, VMEM, VMEM],
        out_specs=[ANY] * len(chunks),
        scratch_shapes=[
            pltpu.VMEM((blocks, depth, PB), jnp.bfloat16),
            pltpu.VMEM((gp, depth), jnp.bfloat16),
            pltpu.VMEM((blocks, blocks, PB, PB), jnp.float32),
            pltpu.SMEM((blocks,), jnp.int32),
            pltpu.SemaphoreType.DMA((bundles,)),
            pltpu.SemaphoreType.DMA,
        ],
        compiler_params=params(52),
        name="region",
    )(ids, resid, local, factor)


def tile_places(sectors, row_index, col_index, n_row, capacity):
    residue, group = sectors % n_row, sectors // n_row
    in_row, in_col = residue == row_index, group == col_index
    has_col = jnp.any(in_col, axis=1, keepdims=True)
    column = jnp.sum(jnp.where(in_col, sectors, 0), axis=1, keepdims=True)
    lower = sectors[:, None, :] < sectors[:, :, None]
    rank = jnp.sum((lower & in_row[:, None, :]).astype(jnp.int32), axis=2)
    same = has_col & (column % n_row == row_index)
    slot = jnp.where(in_col, 0, rank + (same & (sectors < column)).astype(jnp.int32))
    place = group * n_row + column % n_row
    found = in_row & has_col
    return [
        jnp.max(jnp.where(found & (slot == s), place, -1), axis=1) for s in range(capacity)
    ]


def add_tiles(places, arrived, total, first, count):
    @pl.loop(0, arrived.shape[0])
    def _(d):
        place = places[d]

        @pl.when(place >= 0)
        def _():
            total[place, pl.ds(first, count), :] += arrived[d]


def first_kernel(places, where, arrived, damping, total, pivot):
    total[...] = jnp.zeros_like(total)
    add_tiles(places, arrived, total, 0, PB)
    line = lax.broadcasted_iota(jnp.int32, (PB, PB), 0)
    column = lax.broadcasted_iota(jnp.int32, (PB, PB), 1)
    corner = total[where[0]] + jnp.where(line == column, damping[...], 0.0)
    total[where[0]] = corner
    pivot[...] = corner


def first_tiles(places, where, arrived, damping, tiles):
    return pl.pallas_call(
        first_kernel,
        out_shape=[
            jax.ShapeDtypeStruct((tiles, PB, PB), jnp.float32),
            jax.ShapeDtypeStruct((PB, PB), jnp.float32),
        ],
        in_specs=[SMEM, SMEM, VMEM, VMEM],
        out_specs=[VMEM, VMEM],
        compiler_params=params(12),
        name="first_tiles",
    )(places, where, arrived, damping)


def more_kernel(first, count, places, arrived, total_in, total):
    add_tiles(places, arrived, total, first, count)


def more_tiles(places, arrived, total, first, count):
    return pl.pallas_call(
        functools.partial(more_kernel, first, count),
        out_shape=jax.ShapeDtypeStruct(total.shape, jnp.float32),
        in_specs=[SMEM, VMEM, VMEM],
        out_specs=VMEM,
        input_output_aliases={2: 0},
        compiler_params=params(12),
        name="more_tiles",
    )(places, arrived, total)


def products(where, vectors, high, low, both, keep, away):
    n_row = keep.shape[0] * 2
    for mask, vector in enumerate(vectors):
        at = pl.multiple_of((where[2] ^ mask) * PB, PB)
        vh, vl = split(vector[...])
        both[0, :, pl.ds(at, PB)] = vh
        both[1, :, pl.ds(at, PB)] = vl
    result = dot_split((both[0], both[1]), (high[...], low[...]))
    for sub in range(n_row):
        mask = where[1] ^ sub
        part = result[:, sub * PB : (sub + 1) * PB]

        @pl.when(mask % 2 == 0)
        def _():
            keep[mask // 2] = part

        @pl.when(mask % 2 == 1)
        def _():
            away[mask // 2] = part


def finish_kernel(first, count, n_vec, places, where, arrived, total_in, *refs):
    vectors = refs[:n_vec]
    normal, high, low, keep, away, both, total = refs[n_vec:]
    n_row = keep.shape[0] * 2
    if count:
        total[...] = total_in[...]
        add_tiles(places, arrived, total, first, count)
    else:
        total = total_in
    for a in range(n_vec):
        for sub in range(n_row):
            tile = total[a * n_row + sub]
            normal[a, 0, :, sub * PB : (sub + 1) * PB] = tile
            th, tl = split(tile)
            high[a * PB : (a + 1) * PB, sub * PB : (sub + 1) * PB] = th
            low[a * PB : (a + 1) * PB, sub * PB : (sub + 1) * PB] = tl
    products(where, vectors, high, low, both, keep, away)


def finish(places, where, arrived, total, vectors, n_row, first, count):
    n_col = len(vectors)
    wide = vectors[0].shape[0]
    halves = jax.ShapeDtypeStruct((n_row // 2, wide, PB), jnp.float32)
    return pl.pallas_call(
        functools.partial(finish_kernel, first, count, n_col),
        out_shape=[
            jax.ShapeDtypeStruct((n_col, 1, PB, n_row * PB), jnp.float32),
            jax.ShapeDtypeStruct((n_col * PB, n_row * PB), jnp.bfloat16),
            jax.ShapeDtypeStruct((n_col * PB, n_row * PB), jnp.bfloat16),
            halves,
            halves,
        ],
        in_specs=[SMEM, SMEM, VMEM, VMEM] + [VMEM] * n_col,
        out_specs=[VMEM] * 5,
        scratch_shapes=[
            pltpu.VMEM((2, wide, n_col * PB), jnp.bfloat16),
            pltpu.VMEM(total.shape, jnp.float32),
        ],
        compiler_params=params(24),
        name="finish",
    )(places, where, arrived, total, *vectors)


def apply_kernel(n_vec, where, high, low, *refs):
    vectors = refs[:n_vec]
    keep, away, both = refs[n_vec:]
    products(where, vectors, high, low, both, keep, away)


def apply_matrix(where, high, low, vectors, n_row):
    n_col = len(vectors)
    wide = vectors[0].shape[0]
    halves = jax.ShapeDtypeStruct((n_row // 2, wide, PB), jnp.float32)
    return pl.pallas_call(
        functools.partial(apply_kernel, n_col),
        out_shape=[halves, halves],
        in_specs=[SMEM, VMEM, VMEM] + [VMEM] * n_col,
        out_specs=[VMEM] * 2,
        scratch_shapes=[pltpu.VMEM((2, wide, n_col * PB), jnp.bfloat16)],
        compiler_params=params(12),
        name="apply_matrix",
    )(where, high, low, *vectors)


def swap(x, axis, mask):
    return lax.ppermute(x, axis, [(i, i ^ mask) for i in range(lax.axis_size(axis))])


def gather_columns(own):
    half = lax.axis_size("col") // 2
    far = swap(own, "col", half)
    near = [own] + [swap(own, "col", mask) for mask in range(1, half)]
    beyond = [far] + [swap(far, "col", mask) for mask in range(1, half)]
    return near + beyond


def sum_rows(keep, away):
    mask = 1
    while True:
        summed = keep + swap(away, "row", mask)
        mask *= 2
        if mask == lax.axis_size("row"):
            return summed[0]
        keep, away = summed[0::2], summed[1::2]


def exchange(x):
    return lax.all_to_all(x, BOTH, split_axis=0, concat_axis=0, tiled=True)


def body(resid_deriv, local_deriv, inv_factor, block_ids, right_sides, damping):
    n_row, n_col = lax.axis_size("row"), lax.axis_size("col")
    devices = n_row * n_col
    capacity = max(block_ids.shape[1] // n_row, 1)
    chunks = chunk_list(capacity)
    row_index, col_index = lax.axis_index("row"), lax.axis_index("col")
    where = jnp.stack([col_index * n_row + row_index, row_index, col_index]).astype(jnp.int32)

    sends = region(block_ids, resid_deriv, local_deriv, inv_factor, n_row, n_col, chunks)
    arrived = []
    for x in sends:
        arrived.append(exchange(x))
    sectors = exchange(jnp.broadcast_to(block_ids[:1], (devices, block_ids.shape[1])))
    places = tile_places(sectors, row_index, col_index, n_row, capacity)

    total, pivot = first_tiles(places[0], where, arrived[0], damping[None, :], devices)
    factor = lax.linalg.cholesky(pivot)
    inverse_factor = lax.linalg.triangular_solve(
        factor, jnp.eye(PB, dtype=jnp.float32), left_side=True, lower=True
    )
    high_dot = functools.partial(jnp.dot, precision=lax.Precision.HIGHEST)
    inverse = high_dot(inverse_factor.T, inverse_factor)
    residual = right_sides.T
    update = high_dot(residual, inverse) / center
    vectors = gather_columns(update)

    for (slot, first, count), x in list(zip(chunks, arrived))[1:-1]:
        total = more_tiles(places[slot], x, total, first, count)
    slot, first, count = chunks[-1]
    normal, high, low, keep, away = finish(
        places[slot], where, arrived[-1], total, vectors, n_row, first, count if len(chunks) > 1 else 0
    )
    answer = update
    weight = 1.0 / ratio
    for sweep in range(1, ITERS):
        residual = residual - sum_rows(keep, away)
        weight_next = 1.0 / (2.0 * ratio - weight)
        update = weight_next * weight * update + 2.0 * weight_next / radius * high_dot(
            residual, inverse
        )
        weight = weight_next
        answer = answer + update
        if sweep + 1 < ITERS:
            vectors = gather_columns(update)
            keep, away = apply_matrix(where, high, low, vectors, n_row)
    return normal, answer.T


def solution(mesh):
    return jax.shard_map(
        body,
        mesh=mesh,
        in_specs=(
            P(BOTH, None, None),
            P(BOTH, None, None),
            P(BOTH, None, None),
            P(BOTH, None),
            P(("col", "row"), None),
            P(("col", "row")),
        ),
        out_specs=(P(None, "row", None, "col"), P(("col", "row"), None)),
        check_vma=False,
    )
```

```python
import functools

import jax
import jax.numpy as jnp
from jax import lax
from jax.experimental import pallas as pl
from jax.experimental.pallas import tpu as pltpu
from jax.sharding import PartitionSpec as P


PB = 128
ITERS = 3

cheb_low = 0.05
cheb_high = 2.0
center = (cheb_high + cheb_low) / 2.0
radius = (cheb_high - cheb_low) / 2.0
ratio = center / radius

BOTH = ("row", "col")
VMEM = pl.BlockSpec(memory_space=pltpu.VMEM)
SMEM = pl.BlockSpec(memory_space=pltpu.SMEM)
ANY = pl.BlockSpec(memory_space=pl.ANY)
HBM = pl.BlockSpec(memory_space=pltpu.HBM)
f32_dot = functools.partial(jnp.dot, preferred_element_type=jnp.float32)


def params(mib):
    return pltpu.CompilerParams(vmem_limit_bytes=mib << 20)


def split(x):
    high = x.astype(jnp.bfloat16)
    return high, (x - high.astype(jnp.float32)).astype(jnp.bfloat16)


def dot_split(a, b):
    (ah, al), (bh, bl) = a, b
    return f32_dot(ah, bh) + (f32_dot(ah, bl) + f32_dot(al, bh))


def chunk_list(capacity):
    chunks = [(0, 0, PB + 8)]
    for slot in range(1, capacity):
        chunks += [(slot, 0, PB // 2), (slot, PB // 2, PB // 2)]
    return chunks


def region_kernel(n_row, n_col, chunks, ids_in, resid, local_in, factor_in, *refs):
    outs = refs[: len(chunks)]
    bundles, _, gp = resid.shape
    blocks, n = gp // PB, factor_in.shape[2]
    refs = refs[len(chunks) :]
    cols, rows, coupled = refs[:bundles], refs[bundles : 2 * bundles], refs[2 * bundles :][:2]
    ids, raw, down, across, local, factor, stage, sector, in_sem, small_sem, out_sem = refs[
        2 * bundles + 2 :
    ]

    fetch_ids = pltpu.make_async_copy(ids_in, ids, small_sem.at[0])
    fetch_local = pltpu.make_async_copy(local_in, local, small_sem.at[1])
    fetch_factor = pltpu.make_async_copy(factor_in, factor, small_sem.at[2])
    fetch_ids.start()
    fetch_local.start()
    fetch_factor.start()
    fetches = [
        pltpu.make_async_copy(resid.at[b], raw.at[b], in_sem.at[b]) for b in range(bundles)
    ]
    for fetch in fetches:
        fetch.start()
    stage[0, :, PB:, :] = jnp.full((n_row * n_col, 8, PB), -1.0, jnp.float32)
    fetch_ids.wait()
    fetch_local.wait()
    fetch_factor.wait()

    def arrange(b):
        fetches[b].wait()
        for k in range(blocks):
            rank = jnp.int32(0)
            for j in range(blocks):
                if j != k:
                    rank = rank + (ids[b, j] < ids[b, k]).astype(jnp.int32)
            if b == 0:
                sector[rank] = ids[b, k]
            block = raw[b, :, k * PB : (k + 1) * PB]
            cols[b][rank] = block
            rows[b][pl.ds(pl.multiple_of(rank * PB, PB), PB), :] = block.T

    def couple(b):
        coupled[b % 2][...] = f32_dot(rows[b][...], local[b])

    def project(b):
        ch, cl = split(coupled[b % 2][...])
        fh, fl = split(factor[b])
        terms = jnp.concatenate([fh, fl], axis=1)
        parts = f32_dot(jnp.concatenate([ch, cl], axis=1), jnp.concatenate([terms, terms], axis=0))
        projected = (parts[:, :n] + parts[:, n:]).astype(jnp.bfloat16)
        across[:, b * n : (b + 1) * n] = -projected
        for p in range(blocks):
            down[p, b * n : (b + 1) * n, :] = projected[p * PB : (p + 1) * PB].T

    for step in range(bundles + 2):
        if step >= 2:
            project(step - 2)
        if 1 <= step <= bundles:
            couple(step - 1)
        if step < bundles:
            arrange(step)

    def left(i):
        parts = [r[i * PB : (i + 2) * PB, :] for r in rows] + [across[i * PB : (i + 2) * PB, :]]
        return jnp.concatenate(parts, axis=1)

    def right(j):
        pair = [[c[j + x] for c in cols] + [down[j + x]] for x in range(2)]
        return jnp.concatenate([jnp.concatenate(x, axis=0) for x in pair], axis=1)

    def put(g, h, tile):
        mine, other = sector[g], sector[h]
        residue = lax.rem(mine, n_row)
        slot = jnp.int32(0)
        if g != h:
            for j in range(g):
                slot = slot + (lax.rem(sector[j], n_row) == residue).astype(jnp.int32)
        if g < h:
            slot = slot + (lax.rem(other, n_row) == residue).astype(jnp.int32)
        owner = residue * n_col + lax.div(other, n_row)
        stage[slot, owner, :PB, :] = tile
        place = mine - residue + lax.rem(other, n_row)
        stage[0, owner, pl.ds(PB + slot, 1), :] = jnp.full((1, PB), place.astype(jnp.float32))

    for i in range(0, blocks, 2):
        for j in range(i, blocks, 2):
            total = f32_dot(left(i), right(j))
            for x in range(2):
                for y in range(2):
                    tile = total[x * PB : (x + 1) * PB, y * PB : (y + 1) * PB]
                    put(i + x, j + y, tile)
                    if i != j:
                        put(j + y, i + x, tile.T)
    copies = [
        pltpu.make_async_copy(stage.at[slot, :, pl.ds(first, count), :], out, out_sem.at[i])
        for i, (out, (slot, first, count)) in enumerate(zip(outs, chunks))
    ]
    for copy in copies:
        copy.start()
    for copy in copies:
        copy.wait()


def region(ids, resid, local, factor, n_row, n_col, capacity, chunks):
    bundles, m, gp = resid.shape
    blocks, n = ids.shape[1], local.shape[2]
    return pl.pallas_call(
        functools.partial(region_kernel, n_row, n_col, chunks),
        out_shape=[
            jax.ShapeDtypeStruct((n_row * n_col, count, PB), jnp.float32) for _, _, count in chunks
        ],
        in_specs=[HBM] * 4,
        out_specs=[HBM] * len(chunks),
        scratch_shapes=[pltpu.VMEM((blocks, m, PB), jnp.bfloat16)] * bundles
        + [pltpu.VMEM((gp, m), jnp.bfloat16)] * bundles
        + [pltpu.VMEM((gp, n), jnp.float32)] * 2
        + [
            pltpu.SMEM(ids.shape, jnp.int32),
            pltpu.VMEM(resid.shape, resid.dtype),
            pltpu.VMEM((blocks, bundles * n, PB), jnp.bfloat16),
            pltpu.VMEM((gp, bundles * n), jnp.bfloat16),
            pltpu.VMEM(local.shape, local.dtype),
            pltpu.VMEM(factor.shape, factor.dtype),
            pltpu.VMEM((capacity, n_row * n_col, PB + 8, PB), jnp.float32),
            pltpu.SMEM((blocks,), jnp.int32),
            pltpu.SemaphoreType.DMA((bundles,)),
            pltpu.SemaphoreType.DMA((3,)),
            pltpu.SemaphoreType.DMA((len(chunks),)),
        ],
        compiler_params=params(48),
        name="region",
    )(ids, resid, local, factor)


def add_tiles(places, slot, arrived, total, first, count):
    def step(d, carry):
        place = places[d, slot]

        @pl.when(place >= 0)
        def _():
            total[place, pl.ds(first, count), :] += arrived[d, :count, :]

        return carry

    lax.fori_loop(0, arrived.shape[0], step, 0)


def first_kernel(where, places, arrived, damping, total, pivot, held, sem):
    fetch = pltpu.make_async_copy(arrived, held, sem)
    fetch.start()
    total[...] = jnp.zeros_like(total)
    fetch.wait()
    add_tiles(places, 0, held, total, 0, PB)
    line = lax.broadcasted_iota(jnp.int32, (PB, PB), 0)
    column = lax.broadcasted_iota(jnp.int32, (PB, PB), 1)
    corner = total[where[0]] + jnp.where(line == column, damping[...], 0.0)
    total[where[0]] = corner
    pivot[...] = corner


def first_tiles(where, places, arrived, damping, tiles):
    return pl.pallas_call(
        first_kernel,
        out_shape=[
            jax.ShapeDtypeStruct((tiles, PB, PB), jnp.float32),
            jax.ShapeDtypeStruct((PB, PB), jnp.float32),
        ],
        in_specs=[SMEM, SMEM, ANY, VMEM],
        out_specs=[VMEM, VMEM],
        scratch_shapes=[pltpu.VMEM(arrived.shape, jnp.float32), pltpu.SemaphoreType.DMA],
        compiler_params=params(24),
        name="first_tiles",
    )(where, places, arrived, damping)


def invert_kernel(factor, rhs, inverse, turned, update):
    line = lax.broadcasted_iota(jnp.int32, (PB, PB), 0)
    column = lax.broadcasted_iota(jnp.int32, (PB, PB), 1)

    def product(a, b):
        return dot_split(split(a), split(b))

    c = jnp.where(line >= column, factor[...], 0.0)
    diagonal = jnp.sum(jnp.where(line == column, c, 0.0), axis=1, keepdims=True)
    scale = 1.0 / diagonal
    unit = c * scale
    eye = jnp.where(line == column, 1.0, 0.0)
    size = 4
    near = jnp.where((line // size == column // size) & (line > column), unit, 0.0)
    second = product(near, near)
    grown = (eye - near) + product(eye - near, second)
    while size < PB:
        size *= 2
        link = jnp.where(
            (line // size == column // size) & (line // (size // 2) != column // (size // 2)), unit, 0.0
        )
        grown = grown - product(product(grown, link), grown)
    across = jnp.sum(jnp.where(line == column, c, 0.0), axis=0, keepdims=True)
    lower = grown * (1.0 / across)
    full = product(lower.T, lower)
    inverse[...] = full
    back = rhs[...].T
    turned[...] = back
    update[...] = product(back, full) / center


def invert(factor, rhs):
    wide = rhs.shape[1]
    return pl.pallas_call(
        invert_kernel,
        out_shape=[
            jax.ShapeDtypeStruct((PB, PB), jnp.float32),
            jax.ShapeDtypeStruct((wide, PB), jnp.float32),
            jax.ShapeDtypeStruct((wide, PB), jnp.float32),
        ],
        in_specs=[VMEM, VMEM],
        out_specs=[VMEM] * 3,
        compiler_params=params(8),
        name="invert",
    )(factor, rhs)


def more_kernel(slot, first, count, places, arrived, total_in, total, held, sem):
    fetch = pltpu.make_async_copy(arrived, held, sem)
    fetch.start()
    fetch.wait()
    add_tiles(places, slot, held, total, first, count)


def more_tiles(places, arrived, total, slot, first, count):
    return pl.pallas_call(
        functools.partial(more_kernel, slot, first, count),
        out_shape=jax.ShapeDtypeStruct(total.shape, jnp.float32),
        in_specs=[SMEM, ANY, VMEM],
        out_specs=VMEM,
        input_output_aliases={2: 0},
        scratch_shapes=[pltpu.VMEM(arrived.shape, jnp.float32), pltpu.SemaphoreType.DMA],
        compiler_params=params(12),
        name="more_tiles",
    )(places, arrived, total)


def products(where, fetches, vectors, high, low, both, keep, away):
    n_row = keep.shape[0] * 2
    for mask, fetch in enumerate(fetches):
        fetch.wait()
        at = pl.multiple_of((where[2] ^ mask) * PB, PB)
        vh, vl = split(vectors[mask])
        both[0, :, pl.ds(at, PB)] = vh
        both[1, :, pl.ds(at, PB)] = vl
    result = dot_split((both[0], both[1]), (high[...], low[...]))
    for sub in range(n_row):
        mask = where[1] ^ sub
        part = result[:, sub * PB : (sub + 1) * PB]

        @pl.when(mask % 2 == 0)
        def _():
            keep[mask // 2] = part

        @pl.when(mask % 2 == 1)
        def _():
            away[mask // 2] = part


def fetch_all(sources, held, sem):
    fetches = [pltpu.make_async_copy(x, held.at[i], sem.at[i]) for i, x in enumerate(sources)]
    for fetch in fetches:
        fetch.start()
    return fetches


def finish_kernel(slot, first, count, n_vec, where, places, arrived, total_in, *refs):
    vectors = refs[:n_vec]
    normal, high, low, keep, away, total, held, gathered, both, whole, in_sem, vec_sem, out_sem = (
        refs[n_vec:]
    )
    n_row = keep.shape[0] * 2
    fetches = fetch_all(vectors, gathered, vec_sem)
    if count:
        fetch = pltpu.make_async_copy(arrived, held, in_sem)
        fetch.start()
        fetch.wait()
        add_tiles(places, slot, held, total, first, count)
    stores = []
    for a in range(n_vec):
        for sub in range(n_row):
            tile = total[a * n_row + sub]
            whole[a, :, sub * PB : (sub + 1) * PB] = tile
            th, tl = split(tile)
            high[a * PB : (a + 1) * PB, sub * PB : (sub + 1) * PB] = th
            low[a * PB : (a + 1) * PB, sub * PB : (sub + 1) * PB] = tl
        stores.append(pltpu.make_async_copy(whole.at[a], normal.at[a, 0], out_sem.at[a]))
        stores[-1].start()
    products(where, fetches, gathered, high, low, both, keep, away)
    for store in stores:
        store.wait()


def finish(where, places, arrived, total, vectors, n_row, slot, first, count):
    n_col = len(vectors)
    wide = vectors[0].shape[0]
    halves = jax.ShapeDtypeStruct((n_row // 2, wide, PB), jnp.float32)
    half = jax.ShapeDtypeStruct((n_col * PB, n_row * PB), jnp.bfloat16)
    return pl.pallas_call(
        functools.partial(finish_kernel, slot, first, count, n_col),
        out_shape=[
            jax.ShapeDtypeStruct((n_col, 1, PB, n_row * PB), jnp.float32),
            half,
            half,
            halves,
            halves,
            jax.ShapeDtypeStruct(total.shape, jnp.float32),
        ],
        in_specs=[SMEM, SMEM, ANY, VMEM] + [ANY] * n_col,
        out_specs=[ANY] + [VMEM] * 5,
        input_output_aliases={3: 5},
        scratch_shapes=[
            pltpu.VMEM(arrived.shape if count else (8, PB), jnp.float32),
            pltpu.VMEM((n_col, wide, PB), jnp.float32),
            pltpu.VMEM((2, wide, n_col * PB), jnp.bfloat16),
            pltpu.VMEM((n_col, PB, n_row * PB), jnp.float32),
            pltpu.SemaphoreType.DMA,
            pltpu.SemaphoreType.DMA((n_col,)),
            pltpu.SemaphoreType.DMA((n_col,)),
        ],
        compiler_params=params(32),
        name="finish",
    )(where, places, arrived, total, *vectors)


def apply_kernel(n_vec, where, high, low, *refs):
    vectors = refs[:n_vec]
    keep, away, gathered, both, vec_sem = refs[n_vec:]
    fetches = fetch_all(vectors, gathered, vec_sem)
    products(where, fetches, gathered, high, low, both, keep, away)


def apply_matrix(where, high, low, vectors, n_row):
    n_col = len(vectors)
    wide = vectors[0].shape[0]
    halves = jax.ShapeDtypeStruct((n_row // 2, wide, PB), jnp.float32)
    return pl.pallas_call(
        functools.partial(apply_kernel, n_col),
        out_shape=[halves, halves],
        in_specs=[SMEM, VMEM, VMEM] + [ANY] * n_col,
        out_specs=[VMEM] * 2,
        scratch_shapes=[
            pltpu.VMEM((n_col, wide, PB), jnp.float32),
            pltpu.VMEM((2, wide, n_col * PB), jnp.bfloat16),
            pltpu.SemaphoreType.DMA((n_col,)),
        ],
        compiler_params=params(12),
        name="apply_matrix",
    )(where, high, low, *vectors)


def swap(x, axis, mask):
    return lax.ppermute(x, axis, [(i, i ^ mask) for i in range(lax.axis_size(axis))])


def gather_columns(own):
    half = lax.axis_size("col") // 2
    far = swap(own, "col", half)
    near = [own] + [swap(own, "col", mask) for mask in range(1, half)]
    beyond = [far] + [swap(far, "col", mask) for mask in range(1, half)]
    return near + beyond


def sum_rows(keep, away):
    mask = 1
    while True:
        summed = keep + swap(away, "row", mask)
        mask *= 2
        if mask == lax.axis_size("row"):
            return summed[0]
        keep, away = summed[0::2], summed[1::2]


def exchange(x):
    return lax.all_to_all(x, BOTH, split_axis=0, concat_axis=0, tiled=True)


def body(resid_deriv, local_deriv, inv_factor, block_ids, right_sides, damping):
    n_row, n_col = lax.axis_size("row"), lax.axis_size("col")
    devices = n_row * n_col
    capacity = max(block_ids.shape[1] // n_row, 1)
    chunks = chunk_list(capacity)
    row_index, col_index = lax.axis_index("row"), lax.axis_index("col")
    where = jnp.stack([col_index * n_row + row_index, row_index, col_index]).astype(jnp.int32)

    sends = region(
        block_ids, resid_deriv, local_deriv, inv_factor, n_row, n_col, capacity, chunks
    )
    arrived = []
    for x in sends:
        arrived.append(exchange(x))
    places = arrived[0][:, PB : PB + capacity, 0].astype(jnp.int32)

    total, pivot = first_tiles(where, places, arrived[0], damping[None, :], devices)
    factor = lax.linalg.cholesky(pivot, symmetrize_input=False)
    inverse, residual, update = invert(factor, right_sides)
    vectors = gather_columns(update)

    for (slot, first, count), x in list(zip(chunks, arrived))[1:-1]:
        total = more_tiles(places, x, total, slot, first, count)
    slot, first, count = chunks[-1]
    normal, high, low, keep, away, _ = finish(
        where, places, arrived[-1], total, vectors, n_row, slot, first, count if slot else 0
    )
    high_dot = functools.partial(jnp.dot, precision=lax.Precision.HIGHEST)
    answer = update
    weight = 1.0 / ratio
    for sweep in range(1, ITERS):
        residual = residual - sum_rows(keep, away)
        weight_next = 1.0 / (2.0 * ratio - weight)
        update = weight_next * weight * update + 2.0 * weight_next / radius * high_dot(
            residual, inverse
        )
        weight = weight_next
        answer = answer + update
        if sweep + 1 < ITERS:
            vectors = gather_columns(update)
            keep, away = apply_matrix(where, high, low, vectors, n_row)
    return normal, answer.T


def solution(mesh):
    return jax.shard_map(
        body,
        mesh=mesh,
        in_specs=(
            P(BOTH, None, None),
            P(BOTH, None, None),
            P(BOTH, None, None),
            P(BOTH, None),
            P(("col", "row"), None),
            P(("col", "row")),
        ),
        out_specs=(P(None, "row", None, "col"), P(("col", "row"), None)),
        check_vma=False,
    )
```

```python
import functools

import jax
import jax.numpy as jnp
from jax import lax
from jax.experimental import pallas as pl
from jax.experimental.pallas import tpu as pltpu
from jax.sharding import PartitionSpec as P


PB = 128
ITERS = 3

cheb_low = 0.05
cheb_high = 2.0
center = (cheb_high + cheb_low) / 2.0
radius = (cheb_high - cheb_low) / 2.0
ratio = center / radius

BOTH = ("row", "col")
VMEM = pl.BlockSpec(memory_space=pltpu.VMEM)
SMEM = pl.BlockSpec(memory_space=pltpu.SMEM)
ANY = pl.BlockSpec(memory_space=pl.ANY)
HBM = pl.BlockSpec(memory_space=pltpu.HBM)
f32_dot = functools.partial(jnp.dot, preferred_element_type=jnp.float32)


def params(mib):
    return pltpu.CompilerParams(vmem_limit_bytes=mib << 20)


def split(x):
    high = x.astype(jnp.bfloat16)
    return high, (x - high.astype(jnp.float32)).astype(jnp.bfloat16)


def dot_split(a, b):
    (ah, al), (bh, bl) = a, b
    return f32_dot(ah, bh) + (f32_dot(ah, bl) + f32_dot(al, bh))


def chunk_list(capacity):
    chunks = [(0, 0, PB + 8)]
    for slot in range(1, capacity):
        chunks.append((slot, 0, PB))
    return chunks


def region_kernel(n_row, n_col, chunks, ids_in, resid, local_in, factor_in, *refs):
    outs = refs[: len(chunks)]
    bundles, _, gp = resid.shape
    blocks, n = gp // PB, factor_in.shape[2]
    refs = refs[len(chunks) :]
    cols, rows, coupled = refs[:bundles], refs[bundles : 2 * bundles], refs[2 * bundles :][:2]
    ids, raw, down, across, local, factor, stage, sector, in_sem, small_sem, out_sem = refs[
        2 * bundles + 2 :
    ]

    fetch_ids = pltpu.make_async_copy(ids_in, ids, small_sem.at[0])
    fetch_local = pltpu.make_async_copy(local_in, local, small_sem.at[1])
    fetch_factor = pltpu.make_async_copy(factor_in, factor, small_sem.at[2])
    fetch_ids.start()
    fetch_local.start()
    fetch_factor.start()
    fetches = [
        pltpu.make_async_copy(resid.at[b], raw.at[b], in_sem.at[b]) for b in range(bundles)
    ]
    for fetch in fetches:
        fetch.start()
    stage[0, :, PB:, :] = jnp.full((n_row * n_col, 8, PB), -1.0, jnp.float32)
    fetch_ids.wait()
    fetch_local.wait()
    fetch_factor.wait()

    def arrange(b):
        fetches[b].wait()
        for k in range(blocks):
            rank = jnp.int32(0)
            for j in range(blocks):
                if j != k:
                    rank = rank + (ids[b, j] < ids[b, k]).astype(jnp.int32)
            if b == 0:
                sector[rank] = ids[b, k]
            block = raw[b, :, k * PB : (k + 1) * PB]
            cols[b][rank] = block
            rows[b][pl.ds(pl.multiple_of(rank * PB, PB), PB), :] = block.T

    def couple(b):
        coupled[b % 2][...] = f32_dot(rows[b][...], local[b])

    def project(b):
        ch, cl = split(coupled[b % 2][...])
        fh, fl = split(factor[b])
        terms = jnp.concatenate([fh, fl], axis=1)
        parts = f32_dot(jnp.concatenate([ch, cl], axis=1), jnp.concatenate([terms, terms], axis=0))
        projected = (parts[:, :n] + parts[:, n:]).astype(jnp.bfloat16)
        across[:, b * n : (b + 1) * n] = -projected
        for p in range(blocks):
            down[p, b * n : (b + 1) * n, :] = projected[p * PB : (p + 1) * PB].T

    for step in range(bundles + 2):
        if step >= 2:
            project(step - 2)
        if 1 <= step <= bundles:
            couple(step - 1)
        if step < bundles:
            arrange(step)

    def left(i):
        parts = [r[i * PB : (i + 2) * PB, :] for r in rows] + [across[i * PB : (i + 2) * PB, :]]
        return jnp.concatenate(parts, axis=1)

    def right(j):
        pair = [[c[j + x] for c in cols] + [down[j + x]] for x in range(2)]
        return jnp.concatenate([jnp.concatenate(x, axis=0) for x in pair], axis=1)

    def put(g, h, tile):
        mine, other = sector[g], sector[h]
        residue = lax.rem(mine, n_row)
        slot = jnp.int32(0)
        if g != h:
            for j in range(g):
                slot = slot + (lax.rem(sector[j], n_row) == residue).astype(jnp.int32)
        if g < h:
            slot = slot + (lax.rem(other, n_row) == residue).astype(jnp.int32)
        owner = residue * n_col + lax.div(other, n_row)
        stage[slot, owner, :PB, :] = tile
        place = mine - residue + lax.rem(other, n_row)
        stage[0, owner, pl.ds(PB + slot, 1), :] = jnp.full((1, PB), place.astype(jnp.float32))

    for i in range(0, blocks, 2):
        for j in range(i, blocks, 2):
            total = f32_dot(left(i), right(j))
            for x in range(2):
                for y in range(2):
                    tile = total[x * PB : (x + 1) * PB, y * PB : (y + 1) * PB]
                    put(i + x, j + y, tile)
                    if i != j:
                        put(j + y, i + x, tile.T)
    copies = [
        pltpu.make_async_copy(stage.at[slot, :, pl.ds(first, count), :], out, out_sem.at[i])
        for i, (out, (slot, first, count)) in enumerate(zip(outs, chunks))
    ]
    for copy in copies:
        copy.start()
    for copy in copies:
        copy.wait()


def region(ids, resid, local, factor, n_row, n_col, capacity, chunks):
    bundles, m, gp = resid.shape
    blocks, n = ids.shape[1], local.shape[2]
    return pl.pallas_call(
        functools.partial(region_kernel, n_row, n_col, chunks),
        out_shape=[
            jax.ShapeDtypeStruct((n_row * n_col, count, PB), jnp.float32) for _, _, count in chunks
        ],
        in_specs=[HBM] * 4,
        out_specs=[HBM] * len(chunks),
        scratch_shapes=[pltpu.VMEM((blocks, m, PB), jnp.bfloat16)] * bundles
        + [pltpu.VMEM((gp, m), jnp.bfloat16)] * bundles
        + [pltpu.VMEM((gp, n), jnp.float32)] * 2
        + [
            pltpu.SMEM(ids.shape, jnp.int32),
            pltpu.VMEM(resid.shape, resid.dtype),
            pltpu.VMEM((blocks, bundles * n, PB), jnp.bfloat16),
            pltpu.VMEM((gp, bundles * n), jnp.bfloat16),
            pltpu.VMEM(local.shape, local.dtype),
            pltpu.VMEM(factor.shape, factor.dtype),
            pltpu.VMEM((capacity, n_row * n_col, PB + 8, PB), jnp.float32),
            pltpu.SMEM((blocks,), jnp.int32),
            pltpu.SemaphoreType.DMA((bundles,)),
            pltpu.SemaphoreType.DMA((3,)),
            pltpu.SemaphoreType.DMA((len(chunks),)),
        ],
        compiler_params=params(63),
        name="region",
    )(ids, resid, local, factor)


def add_tiles(places, slot, arrived, total, first, count):
    def step(d, carry):
        place = places[d, slot]

        @pl.when(place >= 0)
        def _():
            total[place, pl.ds(first, count), :] += arrived[d, :count, :]

        return carry

    lax.fori_loop(0, arrived.shape[0], step, 0)


def first_kernel(where, places, arrived, damping, total, pivot, held, sem):
    fetch = pltpu.make_async_copy(arrived, held, sem)
    fetch.start()
    total[...] = jnp.zeros_like(total)
    fetch.wait()
    add_tiles(places, 0, held, total, 0, PB)
    line = lax.broadcasted_iota(jnp.int32, (PB, PB), 0)
    column = lax.broadcasted_iota(jnp.int32, (PB, PB), 1)
    corner = total[where[0]] + jnp.where(line == column, damping[...], 0.0)
    total[where[0]] = corner
    pivot[...] = corner


def first_tiles(where, places, arrived, damping, tiles):
    return pl.pallas_call(
        first_kernel,
        out_shape=[
            jax.ShapeDtypeStruct((tiles, PB, PB), jnp.float32),
            jax.ShapeDtypeStruct((PB, PB), jnp.float32),
        ],
        in_specs=[SMEM, SMEM, ANY, VMEM],
        out_specs=[VMEM, VMEM],
        scratch_shapes=[pltpu.VMEM(arrived.shape, jnp.float32), pltpu.SemaphoreType.DMA],
        compiler_params=params(24),
        name="first_tiles",
    )(where, places, arrived, damping)


def invert_kernel(factor, rhs, inverse, turned, update):
    line = lax.broadcasted_iota(jnp.int32, (PB, PB), 0)
    column = lax.broadcasted_iota(jnp.int32, (PB, PB), 1)

    def product(a, b):
        return dot_split(split(a), split(b))

    c = jnp.where(line >= column, factor[...], 0.0)
    diagonal = jnp.sum(jnp.where(line == column, c, 0.0), axis=1, keepdims=True)
    scale = 1.0 / diagonal
    unit = c * scale
    eye = jnp.where(line == column, 1.0, 0.0)
    size = 4
    near = jnp.where((line // size == column // size) & (line > column), unit, 0.0)
    second = product(near, near)
    grown = (eye - near) + product(eye - near, second)
    while size < PB:
        size *= 2
        link = jnp.where(
            (line // size == column // size) & (line // (size // 2) != column // (size // 2)), unit, 0.0
        )
        grown = grown - product(product(grown, link), grown)
    across = jnp.sum(jnp.where(line == column, c, 0.0), axis=0, keepdims=True)
    lower = grown * (1.0 / across)
    full = product(lower.T, lower)
    inverse[...] = full
    back = rhs[...].T
    turned[...] = back
    update[...] = product(back, full) / center


def invert(factor, rhs):
    wide = rhs.shape[1]
    return pl.pallas_call(
        invert_kernel,
        out_shape=[
            jax.ShapeDtypeStruct((PB, PB), jnp.float32),
            jax.ShapeDtypeStruct((wide, PB), jnp.float32),
            jax.ShapeDtypeStruct((wide, PB), jnp.float32),
        ],
        in_specs=[VMEM, VMEM],
        out_specs=[VMEM] * 3,
        compiler_params=params(8),
        name="invert",
    )(factor, rhs)


def more_kernel(slot, first, count, places, arrived, total_in, total, held, sem):
    fetch = pltpu.make_async_copy(arrived, held, sem)
    fetch.start()
    fetch.wait()
    add_tiles(places, slot, held, total, first, count)


def more_tiles(places, arrived, total, slot, first, count):
    return pl.pallas_call(
        functools.partial(more_kernel, slot, first, count),
        out_shape=jax.ShapeDtypeStruct(total.shape, jnp.float32),
        in_specs=[SMEM, ANY, VMEM],
        out_specs=VMEM,
        input_output_aliases={2: 0},
        scratch_shapes=[pltpu.VMEM(arrived.shape, jnp.float32), pltpu.SemaphoreType.DMA],
        compiler_params=params(12),
        name="more_tiles",
    )(places, arrived, total)


def half_product(where, side, vectors, high, low, both):
    half = len(vectors)
    for mask, vector in enumerate(vectors):
        at = pl.multiple_of((lax.rem(where[2], half) ^ mask) * PB, PB)
        vh, vl = split(vector[...])
        both[0, :, pl.ds(at, PB)] = vh
        both[1, :, pl.ds(at, PB)] = vl
    rows = pl.ds(pl.multiple_of((lax.div(where[2], half) ^ side) * (half * PB), half * PB), half * PB)
    return dot_split((both[0], both[1]), (high[rows, :], low[rows, :]))


def near_kernel(half, where, high, low, *refs):
    vectors, (near, both) = refs[:half], refs[half:]
    near[...] = half_product(where, 0, vectors, high, low, both)


def far_kernel(half, where, near, high, low, *refs):
    vectors, (keep, away, both) = refs[:half], refs[half:]
    result = near[...] + half_product(where, 1, vectors, high, low, both)
    odd = lax.rem(where[1], 2) == 1
    for i in range(keep.shape[0]):
        one = result[:, 2 * i * PB : (2 * i + 1) * PB]
        two = result[:, (2 * i + 1) * PB : (2 * i + 2) * PB]
        at = lax.div(where[1], 2) ^ i
        keep[at] = jnp.where(odd, two, one)
        away[at] = jnp.where(odd, one, two)


def product_scratch(vectors):
    return pltpu.VMEM((2, vectors[0].shape[0], len(vectors) * PB), jnp.bfloat16)


def near_product(where, high, low, vectors):
    return pl.pallas_call(
        functools.partial(near_kernel, len(vectors)),
        out_shape=jax.ShapeDtypeStruct((vectors[0].shape[0], high.shape[1]), jnp.float32),
        in_specs=[SMEM, VMEM, VMEM] + [VMEM] * len(vectors),
        out_specs=VMEM,
        scratch_shapes=[product_scratch(vectors)],
        compiler_params=params(12),
        name="near_product",
    )(where, high, low, *vectors)


def far_product(where, near, high, low, vectors):
    n_row = high.shape[1] // PB
    halves = jax.ShapeDtypeStruct((n_row // 2, vectors[0].shape[0], PB), jnp.float32)
    return pl.pallas_call(
        functools.partial(far_kernel, len(vectors)),
        out_shape=[halves, halves],
        in_specs=[SMEM, VMEM, VMEM, VMEM] + [VMEM] * len(vectors),
        out_specs=[VMEM] * 2,
        scratch_shapes=[product_scratch(vectors)],
        compiler_params=params(12),
        name="far_product",
    )(where, near, high, low, *vectors)


def finish_kernel(slot, first, count, half, where, places, arrived, total_in, *refs):
    vectors = refs[:half]
    normal, high, low, near, total, held, both, whole, in_sem, out_sem = refs[half:]
    n_col, n_row = whole.shape[0], whole.shape[2] // PB
    if count:
        fetch = pltpu.make_async_copy(arrived, held, in_sem)
        fetch.start()
        fetch.wait()
        add_tiles(places, slot, held, total, first, count)
    stores = []
    for a in range(n_col):
        for sub in range(n_row):
            tile = total[a * n_row + sub]
            whole[a, :, sub * PB : (sub + 1) * PB] = tile
            th, tl = split(tile)
            high[a * PB : (a + 1) * PB, sub * PB : (sub + 1) * PB] = th
            low[a * PB : (a + 1) * PB, sub * PB : (sub + 1) * PB] = tl
        stores.append(pltpu.make_async_copy(whole.at[a], normal.at[a, 0], out_sem.at[a]))
        stores[-1].start()
    near[...] = half_product(where, 0, vectors, high, low, both)
    for store in stores:
        store.wait()


def finish(where, places, arrived, total, vectors, n_row, slot, first, count):
    half = len(vectors)
    n_col = 2 * half
    wide = vectors[0].shape[0]
    split_matrix = jax.ShapeDtypeStruct((n_col * PB, n_row * PB), jnp.bfloat16)
    return pl.pallas_call(
        functools.partial(finish_kernel, slot, first, count, half),
        out_shape=[
            jax.ShapeDtypeStruct((n_col, 1, PB, n_row * PB), jnp.float32),
            split_matrix,
            split_matrix,
            jax.ShapeDtypeStruct((wide, n_row * PB), jnp.float32),
            jax.ShapeDtypeStruct(total.shape, jnp.float32),
        ],
        in_specs=[SMEM, SMEM, ANY, VMEM] + [VMEM] * half,
        out_specs=[ANY] + [VMEM] * 4,
        input_output_aliases={3: 4},
        scratch_shapes=[
            pltpu.VMEM(arrived.shape if count else (8, PB), jnp.float32),
            product_scratch(vectors),
            pltpu.VMEM((n_col, PB, n_row * PB), jnp.float32),
            pltpu.SemaphoreType.DMA,
            pltpu.SemaphoreType.DMA((n_col,)),
        ],
        compiler_params=params(24),
        name="finish",
    )(where, places, arrived, total, *vectors)


def swap(x, axis, mask):
    return lax.ppermute(x, axis, [(i, i ^ mask) for i in range(lax.axis_size(axis))])


def gather_columns(own):
    half = lax.axis_size("col") // 2
    far = swap(own, "col", half)
    near = [own] + [swap(own, "col", mask) for mask in range(1, half)]
    beyond = [far] + [swap(far, "col", mask) for mask in range(1, half)]
    return near, beyond


def sum_rows(keep, away):
    mask = 1
    while True:
        summed = keep + swap(away, "row", mask)
        mask *= 2
        if mask == lax.axis_size("row"):
            return summed[0]
        keep, away = summed[0::2], summed[1::2]


def exchange(x):
    return lax.all_to_all(x, BOTH, split_axis=0, concat_axis=0, tiled=True)


def body(resid_deriv, local_deriv, inv_factor, block_ids, right_sides, damping):
    n_row, n_col = lax.axis_size("row"), lax.axis_size("col")
    devices = n_row * n_col
    capacity = max(block_ids.shape[1] // n_row, 1)
    chunks = chunk_list(capacity)
    row_index, col_index = lax.axis_index("row"), lax.axis_index("col")
    where = jnp.stack([col_index * n_row + row_index, row_index, col_index]).astype(jnp.int32)

    sends = region(
        block_ids, resid_deriv, local_deriv, inv_factor, n_row, n_col, capacity, chunks
    )
    arrived = []
    for x in sends:
        arrived.append(exchange(x))
    places = arrived[0][:, PB : PB + capacity, 0].astype(jnp.int32)

    total, pivot = first_tiles(where, places, arrived[0], damping[None, :], devices)
    factor = lax.linalg.cholesky(pivot, symmetrize_input=False)
    inverse, residual, update = invert(factor, right_sides)
    close, beyond = gather_columns(update)

    for (slot, first, count), x in list(zip(chunks, arrived))[1:-1]:
        total = more_tiles(places, x, total, slot, first, count)
    slot, first, count = chunks[-1]
    normal, high, low, near, _ = finish(
        where, places, arrived[-1], total, close, n_row, slot, first, count if slot else 0
    )
    high_dot = functools.partial(jnp.dot, precision=lax.Precision.HIGHEST)
    keep, away = far_product(where, near, high, low, beyond)
    answer = update
    weight = 1.0 / ratio
    for sweep in range(1, ITERS):
        residual = residual - sum_rows(keep, away)
        weight_next = 1.0 / (2.0 * ratio - weight)
        update = weight_next * weight * update + 2.0 * weight_next / radius * high_dot(
            residual, inverse
        )
        weight = weight_next
        answer = answer + update
        if sweep + 1 < ITERS:
            close, beyond = gather_columns(update)
            near = near_product(where, high, low, close)
            keep, away = far_product(where, near, high, low, beyond)
    return normal, answer.T


def solution(mesh):
    return jax.shard_map(
        body,
        mesh=mesh,
        in_specs=(
            P(BOTH, None, None),
            P(BOTH, None, None),
            P(BOTH, None, None),
            P(BOTH, None),
            P(("col", "row"), None),
            P(("col", "row")),
        ),
        out_specs=(P(None, "row", None, "col"), P(("col", "row"), None)),
        check_vma=False,
    )
```

```python
import functools

import jax
import jax.numpy as jnp
from jax import lax
from jax.experimental import pallas as pl
from jax.experimental.pallas import tpu as pltpu
from jax.sharding import PartitionSpec as P


PB = 128
ITERS = 3
AHEAD = 2
LAST = 8

cheb_low = 0.05
cheb_high = 2.0
center = (cheb_high + cheb_low) / 2.0
radius = (cheb_high - cheb_low) / 2.0
ratio = center / radius

BOTH = ("row", "col")
VMEM = pl.BlockSpec(memory_space=pltpu.VMEM)
SMEM = pl.BlockSpec(memory_space=pltpu.SMEM)
ANY = pl.BlockSpec(memory_space=pl.ANY)
HBM = pl.BlockSpec(memory_space=pltpu.HBM)
f32_dot = functools.partial(jnp.dot, preferred_element_type=jnp.float32)


def params(mib):
    return pltpu.CompilerParams(vmem_limit_bytes=mib << 20)


def split(x):
    high = x.astype(jnp.bfloat16)
    return high, (x - high.astype(jnp.float32)).astype(jnp.bfloat16)


def dot_split(a, b):
    (ah, al), (bh, bl) = a, b
    return f32_dot(ah, bh) + (f32_dot(ah, bl) + f32_dot(al, bh))


def region_kernel(n_row, n_col, capacity, ids_in, resid, local_in, factor_in, *refs):
    devices = n_row * n_col
    count = 1 + (capacity - 1) * devices
    outs = refs[:count]
    here = lax.axis_index("row") * n_col + lax.axis_index("col")
    bundles, _, gp = resid.shape
    blocks, n = gp // PB, factor_in.shape[2]
    refs = refs[count:]
    cols, rows, coupled = refs[:bundles], refs[bundles : 2 * bundles], refs[2 * bundles :][:2]
    ids, raw, partial, down, across, local, factor, stage, sector, in_sem, small_sem, out_sem = refs[
        2 * bundles + 2 :
    ]

    fetch_ids = pltpu.make_async_copy(ids_in, ids, small_sem.at[0])
    fetch_local = pltpu.make_async_copy(local_in, local, small_sem.at[1])
    fetch_factor = pltpu.make_async_copy(factor_in, factor, small_sem.at[2])
    fetches = [
        pltpu.make_async_copy(resid.at[b], raw.at[b], in_sem.at[b]) for b in range(bundles)
    ]
    ahead = min(AHEAD, bundles)
    fetch_ids.start()
    for fetch in fetches[:ahead]:
        fetch.start()
    fetch_local.start()
    stage[0, :, PB:, :] = jnp.full((n_row * n_col, 8, PB), -1.0, jnp.float32)
    fetch_ids.wait()

    def arrange(b):
        fetches[b].wait()
        if b == 0:
            fetch_factor.start()
        if b + ahead < bundles:
            fetches[b + ahead].start()
        for k in range(blocks):
            rank = jnp.int32(0)
            for j in range(blocks):
                if j != k:
                    rank = rank + (ids[b, j] < ids[b, k]).astype(jnp.int32)
            if b == 0:
                sector[rank] = ids[b, k]
            block = raw[b, :, k * PB : (k + 1) * PB]
            cols[b][rank] = block
            rows[b][pl.ds(pl.multiple_of(rank * PB, PB), PB), :] = block.T

    def couple(b):
        if b == 0:
            fetch_local.wait()
        coupled[b % 2][...] = f32_dot(rows[b][...], local[b])

    def project(b):
        if b == 0:
            fetch_factor.wait()
        ch, cl = split(coupled[b % 2][...])
        fh, fl = split(factor[b])
        terms = jnp.concatenate([fh, fl], axis=1)
        parts = f32_dot(jnp.concatenate([ch, cl], axis=1), jnp.concatenate([terms, terms], axis=0))
        projected = (parts[:, :n] + parts[:, n:]).astype(jnp.bfloat16)
        across[:, b * n : (b + 1) * n] = -projected
        for p in range(blocks):
            down[p, b * n : (b + 1) * n, :] = projected[p * PB : (p + 1) * PB].T

    def gram(i, j, picked, last):
        left = [rows[b][i * PB : (i + 2) * PB, :] for b in picked]
        pair = [[cols[b][j + x] for b in picked] for x in range(2)]
        if last:
            left.append(across[i * PB : (i + 2) * PB, :])
            pair = [parts + [down[j + x]] for x, parts in enumerate(pair)]
        right = jnp.concatenate([jnp.concatenate(parts, axis=0) for parts in pair], axis=1)
        return f32_dot(jnp.concatenate(left, axis=1), right)

    pairs = [(i, j) for i in range(0, blocks, 2) for j in range(i, blocks, 2)]
    middle = bundles // 2
    steps = bundles + 2
    early = steps - middle
    for step in range(steps):
        if step >= middle:
            for at in range((step - middle) * len(pairs) // early, (step - middle + 1) * len(pairs) // early):
                partial[at] = gram(*pairs[at], range(middle), False)
        if step >= 2:
            project(step - 2)
        if 1 <= step <= bundles:
            couple(step - 1)
        if step < bundles:
            arrange(step)

    def target(g, h):
        mine, other = sector[g], sector[h]
        residue = lax.rem(mine, n_row)
        slot = jnp.int32(0)
        if g != h:
            for j in range(g):
                slot = slot + (lax.rem(sector[j], n_row) == residue).astype(jnp.int32)
        if g < h:
            slot = slot + (lax.rem(other, n_row) == residue).astype(jnp.int32)
        place = mine - residue + lax.rem(other, n_row)
        owner = residue * n_col + lax.div(other, n_row)
        return slot, owner, jnp.where(slot == 0, owner, owner ^ here), place

    def put(g, h, tile):
        slot, owner, index, place = target(g, h)
        stage[slot, index, :PB, :] = tile
        stage[0, owner, pl.ds(PB + slot, 1), :] = jnp.full((1, PB), place.astype(jnp.float32))

    def send(g, h):
        slot, owner, _, _ = target(g, h)

        @pl.when(slot == 0)
        def _():
            pltpu.make_async_copy(
                stage.at[0, owner, pl.ds(0, PB), :], outs[0].at[owner, pl.ds(0, PB), :], out_sem.at[0]
            ).start()

    for at, (i, j) in enumerate(pairs):
        total = partial[at] + gram(i, j, range(middle, bundles), True)
        for x in range(2):
            for y in range(2):
                tile = total[x * PB : (x + 1) * PB, y * PB : (y + 1) * PB]
                put(i + x, j + y, tile)
                if i != j:
                    put(j + y, i + x, tile.T)
        if j + 2 == blocks:
            for x in range(2):
                for h in range(blocks):
                    send(i + x, h)
    marks = pltpu.make_async_copy(
        stage.at[0, :, pl.ds(PB, 8), :], outs[0].at[:, pl.ds(PB, 8), :], out_sem.at[1]
    )
    marks.start()
    for x in range(count - 1):
        pltpu.make_async_copy(
            stage.at[1 + x // devices, x % devices, pl.ds(0, PB), :], outs[1 + x], out_sem.at[2]
        ).start()
    marks.wait()
    sent = stage.at[0, pl.ds(0, blocks * blocks // capacity), pl.ds(0, PB), :]
    pltpu.make_async_copy(sent, sent, out_sem.at[0]).wait()
    if count > 1:
        sent = stage.at[pl.ds(1, capacity - 1), :, pl.ds(0, PB), :]
        pltpu.make_async_copy(sent, sent, out_sem.at[2]).wait()


def region(ids, resid, local, factor, n_row, n_col, capacity):
    bundles, m, gp = resid.shape
    blocks, n = ids.shape[1], local.shape[2]
    return pl.pallas_call(
        functools.partial(region_kernel, n_row, n_col, capacity),
        out_shape=[jax.ShapeDtypeStruct((n_row * n_col, PB + 8, PB), jnp.float32)]
        + [jax.ShapeDtypeStruct((PB, PB), jnp.float32)] * ((capacity - 1) * n_row * n_col),
        in_specs=[HBM] * 4,
        out_specs=[HBM] * (1 + (capacity - 1) * n_row * n_col),
        scratch_shapes=[pltpu.VMEM((blocks, m, PB), jnp.bfloat16)] * bundles
        + [pltpu.VMEM((gp, m), jnp.bfloat16)] * bundles
        + [pltpu.VMEM((gp, n), jnp.float32)] * 2
        + [
            pltpu.SMEM(ids.shape, jnp.int32),
            pltpu.VMEM(resid.shape, resid.dtype),
            pltpu.VMEM((blocks * (blocks + 2) // 8, 2 * PB, 2 * PB), jnp.float32),
            pltpu.VMEM((blocks, bundles * n, PB), jnp.bfloat16),
            pltpu.VMEM((gp, bundles * n), jnp.bfloat16),
            pltpu.VMEM(local.shape, local.dtype),
            pltpu.VMEM(factor.shape, factor.dtype),
            pltpu.VMEM((capacity, n_row * n_col, PB + 8, PB), jnp.float32),
            pltpu.SMEM((blocks,), jnp.int32),
            pltpu.SemaphoreType.DMA((bundles,)),
            pltpu.SemaphoreType.DMA((3,)),
            pltpu.SemaphoreType.DMA((3,)),
        ],
        compiler_params=params(63),
        name="region",
    )(ids, resid, local, factor)


def add_tiles(places, arrived, total):
    def step(d, carry):
        place = places[d, 0]

        @pl.when(place >= 0)
        def _():
            total[place] += arrived[d, :PB, :]

        return carry

    lax.fori_loop(0, arrived.shape[0], step, 0)


def add_singles(where, places, labels, held, total):
    devices = places.shape[0]
    here = where[3]
    for at, x in enumerate(labels):
        place = places[here ^ (x % devices), 1 + x // devices]

        @pl.when(place >= 0)
        def _():
            total[place] += held[at]


def first_kernel(where, places, arrived, damping, total, pivot, held, sem):
    fetch = pltpu.make_async_copy(arrived, held, sem)
    fetch.start()
    total[...] = jnp.zeros_like(total)
    fetch.wait()
    add_tiles(places, held, total)
    line = lax.broadcasted_iota(jnp.int32, (PB, PB), 0)
    column = lax.broadcasted_iota(jnp.int32, (PB, PB), 1)
    corner = total[where[0]] + jnp.where(line == column, damping[...], 0.0)
    total[where[0]] = corner
    pivot[...] = corner


def first_tiles(where, places, arrived, damping, tiles):
    return pl.pallas_call(
        first_kernel,
        out_shape=[
            jax.ShapeDtypeStruct((tiles, PB, PB), jnp.float32),
            jax.ShapeDtypeStruct((PB, PB), jnp.float32),
        ],
        in_specs=[SMEM, SMEM, ANY, VMEM],
        out_specs=[VMEM, VMEM],
        scratch_shapes=[pltpu.VMEM(arrived.shape, jnp.float32), pltpu.SemaphoreType.DMA],
        compiler_params=params(24),
        name="first_tiles",
    )(where, places, arrived, damping)


def invert_kernel(factor, rhs, inverse, turned, update):
    line = lax.broadcasted_iota(jnp.int32, (PB, PB), 0)
    column = lax.broadcasted_iota(jnp.int32, (PB, PB), 1)

    def product(a, b):
        return dot_split(split(a), split(b))

    c = jnp.where(line >= column, factor[...], 0.0)
    diagonal = jnp.sum(jnp.where(line == column, c, 0.0), axis=1, keepdims=True)
    scale = 1.0 / diagonal
    unit = c * scale
    eye = jnp.where(line == column, 1.0, 0.0)
    size = 4
    near = jnp.where((line // size == column // size) & (line > column), unit, 0.0)
    second = product(near, near)
    grown = (eye - near) + product(eye - near, second)
    while size < PB:
        size *= 2
        link = jnp.where(
            (line // size == column // size) & (line // (size // 2) != column // (size // 2)), unit, 0.0
        )
        grown = grown - product(product(grown, link), grown)
    across = jnp.sum(jnp.where(line == column, c, 0.0), axis=0, keepdims=True)
    lower = grown * (1.0 / across)
    full = product(lower.T, lower)
    inverse[...] = full
    back = rhs[...].T
    turned[...] = back
    update[...] = product(back, full) / center


def invert(factor, rhs):
    wide = rhs.shape[1]
    return pl.pallas_call(
        invert_kernel,
        out_shape=[
            jax.ShapeDtypeStruct((PB, PB), jnp.float32),
            jax.ShapeDtypeStruct((wide, PB), jnp.float32),
            jax.ShapeDtypeStruct((wide, PB), jnp.float32),
        ],
        in_specs=[VMEM, VMEM],
        out_specs=[VMEM] * 3,
        compiler_params=params(8),
        name="invert",
    )(factor, rhs)


def more_kernel(labels, where, places, *refs):
    singles, (_, total, held, sem) = refs[: len(labels)], refs[len(labels) :]
    for fetch in fetch_all(singles, held, sem):
        fetch.wait()
    add_singles(where, places, labels, held, total)


def fetch_all(sources, held, sem):
    fetches = [pltpu.make_async_copy(x, held.at[i], sem.at[i]) for i, x in enumerate(sources)]
    for fetch in fetches:
        fetch.start()
    return fetches


def more_tiles(where, places, labels, singles, total):
    return pl.pallas_call(
        functools.partial(more_kernel, labels),
        out_shape=jax.ShapeDtypeStruct(total.shape, jnp.float32),
        in_specs=[SMEM, SMEM] + [ANY] * len(labels) + [VMEM],
        out_specs=VMEM,
        input_output_aliases={2 + len(labels): 0},
        scratch_shapes=[
            pltpu.VMEM((len(labels), PB, PB), jnp.float32),
            pltpu.SemaphoreType.DMA((len(labels),)),
        ],
        compiler_params=params(12),
        name="more_tiles",
    )(where, places, *singles, total)


def half_product(where, side, vectors, high, low, both):
    half = len(vectors)
    for mask, vector in enumerate(vectors):
        at = pl.multiple_of((lax.rem(where[2], half) ^ mask) * PB, PB)
        vh, vl = split(vector[...])
        both[0, :, pl.ds(at, PB)] = vh
        both[1, :, pl.ds(at, PB)] = vl
    rows = pl.ds(pl.multiple_of((lax.div(where[2], half) ^ side) * (half * PB), half * PB), half * PB)
    return dot_split((both[0], both[1]), (high[rows, :], low[rows, :]))


def near_kernel(half, where, high, low, total, *refs):
    vectors, (near, normal, both, whole, sem) = refs[:half], refs[half:]
    n_col, n_row = whole.shape[0], whole.shape[2] // PB
    stores = []
    for a in range(n_col):
        for sub in range(n_row):
            whole[a, :, sub * PB : (sub + 1) * PB] = total[a * n_row + sub]
        stores.append(pltpu.make_async_copy(whole.at[a], normal.at[a, 0], sem.at[a]))
        stores[-1].start()
    near[...] = half_product(where, 0, vectors, high, low, both)
    for store in stores:
        store.wait()


def far_kernel(half, where, near, high, low, *refs):
    vectors, (keep, away, both) = refs[:half], refs[half:]
    result = near[...] + half_product(where, 1, vectors, high, low, both)
    odd = lax.rem(where[1], 2) == 1
    for i in range(keep.shape[0]):
        one = result[:, 2 * i * PB : (2 * i + 1) * PB]
        two = result[:, (2 * i + 1) * PB : (2 * i + 2) * PB]
        at = lax.div(where[1], 2) ^ i
        keep[at] = jnp.where(odd, two, one)
        away[at] = jnp.where(odd, one, two)


def product_scratch(vectors):
    return pltpu.VMEM((2, vectors[0].shape[0], len(vectors) * PB), jnp.bfloat16)


def near_product(where, high, low, total, vectors):
    n_col, n_row = high.shape[0] // PB, high.shape[1] // PB
    return pl.pallas_call(
        functools.partial(near_kernel, len(vectors)),
        out_shape=[
            jax.ShapeDtypeStruct((vectors[0].shape[0], high.shape[1]), jnp.float32),
            jax.ShapeDtypeStruct((n_col, 1, PB, n_row * PB), jnp.float32),
        ],
        in_specs=[SMEM, VMEM, VMEM, VMEM] + [VMEM] * len(vectors),
        out_specs=[VMEM, ANY],
        scratch_shapes=[
            product_scratch(vectors),
            pltpu.VMEM((n_col, PB, n_row * PB), jnp.float32),
            pltpu.SemaphoreType.DMA((n_col,)),
        ],
        compiler_params=params(16),
        name="near_product",
    )(where, high, low, total, *vectors)


def far_product(where, near, high, low, vectors):
    n_row = high.shape[1] // PB
    halves = jax.ShapeDtypeStruct((n_row // 2, vectors[0].shape[0], PB), jnp.float32)
    return pl.pallas_call(
        functools.partial(far_kernel, len(vectors)),
        out_shape=[halves, halves],
        in_specs=[SMEM, VMEM, VMEM, VMEM] + [VMEM] * len(vectors),
        out_specs=[VMEM] * 2,
        scratch_shapes=[product_scratch(vectors)],
        compiler_params=params(12),
        name="far_product",
    )(where, near, high, low, *vectors)


def finish_kernel(labels, half, where, places, total_in, *refs):
    singles, vectors = refs[: len(labels)], refs[len(labels) : len(labels) + half]
    high, low, near, total, held, both, sem, total_sem = refs[len(labels) + half :]
    n_col, n_row = high.shape[0] // PB, high.shape[1] // PB
    bring = pltpu.make_async_copy(total_in, total, total_sem)
    bring.start()
    fetches = fetch_all(singles, held, sem)
    bring.wait()
    for fetch in fetches:
        fetch.wait()
    add_singles(where, places, labels, held, total)
    for a in range(n_col):
        for sub in range(n_row):
            th, tl = split(total[a * n_row + sub])
            high[a * PB : (a + 1) * PB, sub * PB : (sub + 1) * PB] = th
            low[a * PB : (a + 1) * PB, sub * PB : (sub + 1) * PB] = tl
    near[...] = half_product(where, 0, vectors, high, low, both)


def finish(where, places, labels, singles, total, vectors, n_row):
    half = len(vectors)
    n_col = 2 * half
    wide = vectors[0].shape[0]
    slots = max(len(labels), 1)
    split_matrix = jax.ShapeDtypeStruct((n_col * PB, n_row * PB), jnp.bfloat16)
    return pl.pallas_call(
        functools.partial(finish_kernel, labels, half),
        out_shape=[
            split_matrix,
            split_matrix,
            jax.ShapeDtypeStruct((wide, n_row * PB), jnp.float32),
            jax.ShapeDtypeStruct(total.shape, jnp.float32),
        ],
        in_specs=[SMEM, SMEM, ANY] + [ANY] * len(labels) + [VMEM] * half,
        out_specs=[VMEM] * 4,
        scratch_shapes=[
            pltpu.VMEM((slots, PB, PB), jnp.float32),
            product_scratch(vectors),
            pltpu.SemaphoreType.DMA((slots,)),
            pltpu.SemaphoreType.DMA,
        ],
        compiler_params=params(24),
        name="finish",
    )(where, places, total, *singles, *vectors)


def swap(x, axis, mask):
    return lax.ppermute(x, axis, [(i, i ^ mask) for i in range(lax.axis_size(axis))])


def gather_columns(own):
    half = lax.axis_size("col") // 2
    far = swap(own, "col", half)
    near = [own] + [swap(own, "col", mask) for mask in range(1, half)]
    beyond = [far] + [swap(far, "col", mask) for mask in range(1, half)]
    return near, beyond


def sum_rows(keep, away):
    mask = 1
    while True:
        summed = keep + swap(away, "row", mask)
        mask *= 2
        if mask == lax.axis_size("row"):
            return summed[0]
        keep, away = summed[0::2], summed[1::2]


def exchange(x):
    return lax.all_to_all(x, BOTH, split_axis=0, concat_axis=0, tiled=True)


def body(resid_deriv, local_deriv, inv_factor, block_ids, right_sides, damping):
    n_row, n_col = lax.axis_size("row"), lax.axis_size("col")
    devices = n_row * n_col
    capacity = max(block_ids.shape[1] // n_row, 1)
    row_index, col_index = lax.axis_index("row"), lax.axis_index("col")
    where = jnp.stack(
        [col_index * n_row + row_index, row_index, col_index, row_index * n_col + col_index]
    ).astype(jnp.int32)

    sends = region(block_ids, resid_deriv, local_deriv, inv_factor, n_row, n_col, capacity)
    bulk = exchange(sends[0])
    singles = []
    for x, tile in enumerate(sends[1:]):
        if x % devices:
            tile = lax.ppermute(tile, BOTH, [(i, i ^ (x % devices)) for i in range(devices)])
        singles.append(tile)
    places = bulk[:, PB : PB + capacity, 0].astype(jnp.int32)

    total, pivot = first_tiles(where, places, bulk, damping[None, :], devices)
    factor = lax.linalg.cholesky(pivot, symmetrize_input=False)
    inverse, residual, update = invert(factor, right_sides)
    close, beyond = gather_columns(update)

    order = sorted(range(len(singles)), key=lambda x: (x % devices != 0, x))
    soon, late = order[: len(order) - LAST], order[len(order) - LAST :] if order else []
    if soon:
        total = more_tiles(where, places, soon, [singles[x] for x in soon], total)
    high, low, near, total = finish(
        where, places, late, [singles[x] for x in late], total, close, n_row
    )
    high_dot = functools.partial(jnp.dot, precision=lax.Precision.HIGHEST)
    keep, away = far_product(where, near, high, low, beyond)
    answer = update
    weight = 1.0 / ratio
    for sweep in range(1, ITERS):
        residual = residual - sum_rows(keep, away)
        weight_next = 1.0 / (2.0 * ratio - weight)
        update = weight_next * weight * update + 2.0 * weight_next / radius * high_dot(
            residual, inverse
        )
        weight = weight_next
        answer = answer + update
        if sweep + 1 < ITERS:
            close, beyond = gather_columns(update)
            near, normal = near_product(where, high, low, total, close)
            keep, away = far_product(where, near, high, low, beyond)
    return normal, answer.T


def solution(mesh):
    return jax.shard_map(
        body,
        mesh=mesh,
        in_specs=(
            P(BOTH, None, None),
            P(BOTH, None, None),
            P(BOTH, None, None),
            P(BOTH, None),
            P(("col", "row"), None),
            P(("col", "row")),
        ),
        out_specs=(P(None, "row", None, "col"), P(("col", "row"), None)),
        check_vma=False,
    )
```

```python
import functools

import jax
import jax.numpy as jnp
from jax import lax
from jax.experimental import pallas as pl
from jax.experimental.pallas import tpu as pltpu
from jax.sharding import PartitionSpec as P


PB = 128
ITERS = 3
AHEAD = 2
PIECES = 4

cheb_low = 0.05
cheb_high = 2.0
center = (cheb_high + cheb_low) / 2.0
radius = (cheb_high - cheb_low) / 2.0
ratio = center / radius

BOTH = ("row", "col")
VMEM = pl.BlockSpec(memory_space=pltpu.VMEM)
SMEM = pl.BlockSpec(memory_space=pltpu.SMEM)
ANY = pl.BlockSpec(memory_space=pl.ANY)
HBM = pl.BlockSpec(memory_space=pltpu.HBM)
f32_dot = functools.partial(jnp.dot, preferred_element_type=jnp.float32)


def params(mib):
    return pltpu.CompilerParams(vmem_limit_bytes=mib << 20)


def split(x):
    high = x.astype(jnp.bfloat16)
    return high, (x - high.astype(jnp.float32)).astype(jnp.bfloat16)


def dot_split(a, b):
    (ah, al), (bh, bl) = a, b
    return f32_dot(ah, bh) + (f32_dot(ah, bl) + f32_dot(al, bh))


def chunk_list(capacity):
    chunks = [(0, 0, PB + 8)]
    for slot in range(1, capacity):
        chunks.append((slot, 0, PB))
    return chunks


def region_kernel(n_row, n_col, capacity, chunks, ids_in, resid, local_in, factor_in, *refs):
    outs = refs[: len(chunks)]
    bundles, _, gp = resid.shape
    blocks, n = gp // PB, factor_in.shape[2]
    refs = refs[len(chunks) :]
    cols, rows, coupled = refs[:bundles], refs[bundles : 2 * bundles], refs[2 * bundles :][:2]
    ids, raw, partial, down, across, local, factor, stage, sector, in_sem, small_sem, out_sem = refs[
        2 * bundles + 2 :
    ]

    fetch_ids = pltpu.make_async_copy(ids_in, ids, small_sem.at[0])
    fetch_local = pltpu.make_async_copy(local_in, local, small_sem.at[1])
    fetch_factor = pltpu.make_async_copy(factor_in, factor, small_sem.at[2])
    fetches = [
        pltpu.make_async_copy(resid.at[b], raw.at[b], in_sem.at[b]) for b in range(bundles)
    ]
    ahead = min(AHEAD, bundles)
    fetch_ids.start()
    for fetch in fetches[:ahead]:
        fetch.start()
    fetch_local.start()
    stage[0, :, PB:, :] = jnp.full((n_row * n_col, 8, PB), -1.0, jnp.float32)
    fetch_ids.wait()

    def arrange(b):
        fetches[b].wait()
        if b == 0:
            fetch_factor.start()
        if b + ahead < bundles:
            fetches[b + ahead].start()
        for k in range(blocks):
            rank = jnp.int32(0)
            for j in range(blocks):
                if j != k:
                    rank = rank + (ids[b, j] < ids[b, k]).astype(jnp.int32)
            if b == 0:
                sector[rank] = ids[b, k]
            block = raw[b, :, k * PB : (k + 1) * PB]
            cols[b][rank] = block
            rows[b][pl.ds(pl.multiple_of(rank * PB, PB), PB), :] = block.T

    def couple(b):
        if b == 0:
            fetch_local.wait()
        coupled[b % 2][...] = f32_dot(rows[b][...], local[b])

    def project(b):
        if b == 0:
            fetch_factor.wait()
        ch, cl = split(coupled[b % 2][...])
        fh, fl = split(factor[b])
        terms = jnp.concatenate([fh, fl], axis=1)
        parts = f32_dot(jnp.concatenate([ch, cl], axis=1), jnp.concatenate([terms, terms], axis=0))
        projected = (parts[:, :n] + parts[:, n:]).astype(jnp.bfloat16)
        across[:, b * n : (b + 1) * n] = -projected
        for p in range(blocks):
            down[p, b * n : (b + 1) * n, :] = projected[p * PB : (p + 1) * PB].T

    def gram(i, j, picked, last):
        left = [rows[b][i * PB : (i + 2) * PB, :] for b in picked]
        pair = [[cols[b][j + x] for b in picked] for x in range(2)]
        if last:
            left.append(across[i * PB : (i + 2) * PB, :])
            pair = [parts + [down[j + x]] for x, parts in enumerate(pair)]
        right = jnp.concatenate([jnp.concatenate(parts, axis=0) for parts in pair], axis=1)
        return f32_dot(jnp.concatenate(left, axis=1), right)

    pairs = [(i, j) for i in range(0, blocks, 2) for j in range(i, blocks, 2)]
    middle = bundles // 2
    steps = bundles + 2
    early = steps - middle
    for step in range(steps):
        if step >= middle:
            for at in range((step - middle) * len(pairs) // early, (step - middle + 1) * len(pairs) // early):
                partial[at] = gram(*pairs[at], range(middle), False)
        if step < bundles:
            arrange(step)
        if 1 <= step <= bundles:
            couple(step - 1)
        if step >= 2:
            project(step - 2)

    def target(g, h):
        mine, other = sector[g], sector[h]
        residue = lax.rem(mine, n_row)
        slot = jnp.int32(0)
        if g != h:
            for j in range(g):
                slot = slot + (lax.rem(sector[j], n_row) == residue).astype(jnp.int32)
        if g < h:
            slot = slot + (lax.rem(other, n_row) == residue).astype(jnp.int32)
        place = mine - residue + lax.rem(other, n_row)
        return slot, residue * n_col + lax.div(other, n_row), place

    def put(g, h, tile):
        slot, owner, place = target(g, h)
        stage[slot, owner, :PB, :] = tile
        stage[0, owner, pl.ds(PB + slot, 1), :] = jnp.full((1, PB), place.astype(jnp.float32))

    def send(g, h):
        slot, owner, _ = target(g, h)
        tile = stage.at[slot, owner, pl.ds(0, PB), :]
        for out, (at_slot, _, _) in zip(outs, chunks):

            @pl.when(slot == at_slot)
            def _():
                there = out.at[owner, pl.ds(0, PB), :]
                pltpu.make_async_copy(tile, there, out_sem.at[0]).start()

    for at, (i, j) in enumerate(pairs):
        total = partial[at] + gram(i, j, range(middle, bundles), True)
        for x in range(2):
            for y in range(2):
                tile = total[x * PB : (x + 1) * PB, y * PB : (y + 1) * PB]
                put(i + x, j + y, tile)
                if i != j:
                    put(j + y, i + x, tile.T)
        if j + 2 == blocks:
            for x in range(2):
                for h in range(blocks):
                    send(i + x, h)
    marks = pltpu.make_async_copy(
        stage.at[0, :, pl.ds(PB, 8), :], outs[0].at[:, pl.ds(PB, 8), :], out_sem.at[1]
    )
    marks.start()
    marks.wait()
    sent = stage.at[:, pl.ds(0, blocks * blocks // capacity), pl.ds(0, PB), :]
    pltpu.make_async_copy(sent, sent, out_sem.at[0]).wait()


def region(ids, resid, local, factor, n_row, n_col, capacity, chunks):
    bundles, m, gp = resid.shape
    blocks, n = ids.shape[1], local.shape[2]
    return pl.pallas_call(
        functools.partial(region_kernel, n_row, n_col, capacity, chunks),
        out_shape=[
            jax.ShapeDtypeStruct((n_row * n_col, count, PB), jnp.float32) for _, _, count in chunks
        ],
        in_specs=[HBM] * 4,
        out_specs=[HBM] * len(chunks),
        scratch_shapes=[pltpu.VMEM((blocks, m, PB), jnp.bfloat16)] * bundles
        + [pltpu.VMEM((gp, m), jnp.bfloat16)] * bundles
        + [pltpu.VMEM((gp, n), jnp.float32)] * 2
        + [
            pltpu.SMEM(ids.shape, jnp.int32),
            pltpu.VMEM(resid.shape, resid.dtype),
            pltpu.VMEM((blocks * (blocks + 2) // 8, 2 * PB, 2 * PB), jnp.float32),
            pltpu.VMEM((blocks, bundles * n, PB), jnp.bfloat16),
            pltpu.VMEM((gp, bundles * n), jnp.bfloat16),
            pltpu.VMEM(local.shape, local.dtype),
            pltpu.VMEM(factor.shape, factor.dtype),
            pltpu.VMEM((capacity, n_row * n_col, PB + 8, PB), jnp.float32),
            pltpu.SMEM((blocks,), jnp.int32),
            pltpu.SemaphoreType.DMA((bundles,)),
            pltpu.SemaphoreType.DMA((3,)),
            pltpu.SemaphoreType.DMA((2,)),
        ],
        compiler_params=params(63),
        name="region",
    )(ids, resid, local, factor)


def add_tiles(places, slot, arrived, total, first, count, start=0, size=None):
    def step(d, carry):
        place = places[d, slot]

        @pl.when(place >= 0)
        def _():
            total[place, pl.ds(first, count), :] += arrived[d, :count, :]

        return carry

    lax.fori_loop(start, start + (size or arrived.shape[0]), step, 0)


def first_kernel(where, places, arrived, damping, total, pivot, held, sem):
    fetch = pltpu.make_async_copy(arrived, held, sem)
    fetch.start()
    total[...] = jnp.zeros_like(total)
    fetch.wait()
    add_tiles(places, 0, held, total, 0, PB)
    line = lax.broadcasted_iota(jnp.int32, (PB, PB), 0)
    column = lax.broadcasted_iota(jnp.int32, (PB, PB), 1)
    corner = total[where[0]] + jnp.where(line == column, damping[...], 0.0)
    total[where[0]] = corner
    pivot[...] = corner


def first_tiles(where, places, arrived, damping, tiles):
    return pl.pallas_call(
        first_kernel,
        out_shape=[
            jax.ShapeDtypeStruct((tiles, PB, PB), jnp.float32),
            jax.ShapeDtypeStruct((PB, PB), jnp.float32),
        ],
        in_specs=[SMEM, SMEM, ANY, VMEM],
        out_specs=[VMEM, VMEM],
        scratch_shapes=[pltpu.VMEM(arrived.shape, jnp.float32), pltpu.SemaphoreType.DMA],
        compiler_params=params(24),
        name="first_tiles",
    )(where, places, arrived, damping)


def invert_kernel(factor, rhs, inverse, turned, update):
    line = lax.broadcasted_iota(jnp.int32, (PB, PB), 0)
    column = lax.broadcasted_iota(jnp.int32, (PB, PB), 1)

    def product(a, b):
        return dot_split(split(a), split(b))

    c = jnp.where(line >= column, factor[...], 0.0)
    diagonal = jnp.sum(jnp.where(line == column, c, 0.0), axis=1, keepdims=True)
    scale = 1.0 / diagonal
    unit = c * scale
    eye = jnp.where(line == column, 1.0, 0.0)
    size = 4
    near = jnp.where((line // size == column // size) & (line > column), unit, 0.0)
    second = product(near, near)
    grown = (eye - near) + product(eye - near, second)
    while size < PB:
        size *= 2
        link = jnp.where(
            (line // size == column // size) & (line // (size // 2) != column // (size // 2)), unit, 0.0
        )
        grown = grown - product(product(grown, link), grown)
    across = jnp.sum(jnp.where(line == column, c, 0.0), axis=0, keepdims=True)
    lower = grown * (1.0 / across)
    full = product(lower.T, lower)
    inverse[...] = full
    back = rhs[...].T
    turned[...] = back
    update[...] = product(back, full) / center


def invert(factor, rhs):
    wide = rhs.shape[1]
    return pl.pallas_call(
        invert_kernel,
        out_shape=[
            jax.ShapeDtypeStruct((PB, PB), jnp.float32),
            jax.ShapeDtypeStruct((wide, PB), jnp.float32),
            jax.ShapeDtypeStruct((wide, PB), jnp.float32),
        ],
        in_specs=[VMEM, VMEM],
        out_specs=[VMEM] * 3,
        compiler_params=params(8),
        name="invert",
    )(factor, rhs)


def more_kernel(slot, first, count, places, arrived, total_in, total, held, sem):
    fetch = pltpu.make_async_copy(arrived, held, sem)
    fetch.start()
    fetch.wait()
    add_tiles(places, slot, held, total, first, count)


def more_tiles(places, arrived, total, slot, first, count):
    return pl.pallas_call(
        functools.partial(more_kernel, slot, first, count),
        out_shape=jax.ShapeDtypeStruct(total.shape, jnp.float32),
        in_specs=[SMEM, ANY, VMEM],
        out_specs=VMEM,
        input_output_aliases={2: 0},
        scratch_shapes=[pltpu.VMEM(arrived.shape, jnp.float32), pltpu.SemaphoreType.DMA],
        compiler_params=params(12),
        name="more_tiles",
    )(places, arrived, total)


def half_product(where, side, vectors, high, low, both):
    half = len(vectors)
    for mask, vector in enumerate(vectors):
        at = pl.multiple_of((lax.rem(where[2], half) ^ mask) * PB, PB)
        vh, vl = split(vector[...])
        both[0, :, pl.ds(at, PB)] = vh
        both[1, :, pl.ds(at, PB)] = vl
    rows = pl.ds(pl.multiple_of((lax.div(where[2], half) ^ side) * (half * PB), half * PB), half * PB)
    return dot_split((both[0], both[1]), (high[rows, :], low[rows, :]))


def near_kernel(half, where, high, low, total, *refs):
    vectors, (near, normal, both, whole, sem) = refs[:half], refs[half:]
    n_col, n_row = whole.shape[0], whole.shape[2] // PB
    stores = []
    for a in range(n_col):
        for sub in range(n_row):
            whole[a, :, sub * PB : (sub + 1) * PB] = total[a * n_row + sub]
        stores.append(pltpu.make_async_copy(whole.at[a], normal.at[a, 0], sem.at[a]))
        stores[-1].start()
    near[...] = half_product(where, 0, vectors, high, low, both)
    for store in stores:
        store.wait()


def far_kernel(half, where, near, high, low, *refs):
    vectors, (keep, away, both) = refs[:half], refs[half:]
    result = near[...] + half_product(where, 1, vectors, high, low, both)
    odd = lax.rem(where[1], 2) == 1
    for i in range(keep.shape[0]):
        one = result[:, 2 * i * PB : (2 * i + 1) * PB]
        two = result[:, (2 * i + 1) * PB : (2 * i + 2) * PB]
        at = lax.div(where[1], 2) ^ i
        keep[at] = jnp.where(odd, two, one)
        away[at] = jnp.where(odd, one, two)


def product_scratch(vectors):
    return pltpu.VMEM((2, vectors[0].shape[0], len(vectors) * PB), jnp.bfloat16)


def near_product(where, high, low, total, vectors):
    n_col, n_row = high.shape[0] // PB, high.shape[1] // PB
    return pl.pallas_call(
        functools.partial(near_kernel, len(vectors)),
        out_shape=[
            jax.ShapeDtypeStruct((vectors[0].shape[0], high.shape[1]), jnp.float32),
            jax.ShapeDtypeStruct((n_col, 1, PB, n_row * PB), jnp.float32),
        ],
        in_specs=[SMEM, VMEM, VMEM, VMEM] + [VMEM] * len(vectors),
        out_specs=[VMEM, ANY],
        scratch_shapes=[
            product_scratch(vectors),
            pltpu.VMEM((n_col, PB, n_row * PB), jnp.float32),
            pltpu.SemaphoreType.DMA((n_col,)),
        ],
        compiler_params=params(16),
        name="near_product",
    )(where, high, low, total, *vectors)


def far_product(where, near, high, low, vectors):
    n_row = high.shape[1] // PB
    halves = jax.ShapeDtypeStruct((n_row // 2, vectors[0].shape[0], PB), jnp.float32)
    return pl.pallas_call(
        functools.partial(far_kernel, len(vectors)),
        out_shape=[halves, halves],
        in_specs=[SMEM, VMEM, VMEM, VMEM] + [VMEM] * len(vectors),
        out_specs=[VMEM] * 2,
        scratch_shapes=[product_scratch(vectors)],
        compiler_params=params(12),
        name="far_product",
    )(where, near, high, low, *vectors)


def finish_kernel(slot, first, count, half, where, places, arrived, total_in, *refs):
    vectors = refs[:half]
    high, low, near, total, held, both, in_sem, total_sem = refs[half:]
    n_col, n_row = high.shape[0] // PB, high.shape[1] // PB
    bring = pltpu.make_async_copy(total_in, total, total_sem)
    bring.start()
    pieces = PIECES if count else 0
    size = held.shape[0] // PIECES
    fetches = [
        pltpu.make_async_copy(
            arrived.at[pl.ds(p * size, size)], held.at[pl.ds(p * size, size)], in_sem.at[p]
        )
        for p in range(pieces)
    ]
    for fetch in fetches:
        fetch.start()
    bring.wait()
    for p, fetch in enumerate(fetches):
        fetch.wait()
        add_tiles(places, slot, held, total, first, count, p * size, size)
    for a in range(n_col):
        for sub in range(n_row):
            th, tl = split(total[a * n_row + sub])
            high[a * PB : (a + 1) * PB, sub * PB : (sub + 1) * PB] = th
            low[a * PB : (a + 1) * PB, sub * PB : (sub + 1) * PB] = tl
    near[...] = half_product(where, 0, vectors, high, low, both)


def finish(where, places, arrived, total, vectors, n_row, slot, first, count):
    half = len(vectors)
    n_col = 2 * half
    wide = vectors[0].shape[0]
    split_matrix = jax.ShapeDtypeStruct((n_col * PB, n_row * PB), jnp.bfloat16)
    return pl.pallas_call(
        functools.partial(finish_kernel, slot, first, count, half),
        out_shape=[
            split_matrix,
            split_matrix,
            jax.ShapeDtypeStruct((wide, n_row * PB), jnp.float32),
            jax.ShapeDtypeStruct(total.shape, jnp.float32),
        ],
        in_specs=[SMEM, SMEM, ANY, ANY] + [VMEM] * half,
        out_specs=[VMEM] * 4,
        scratch_shapes=[
            pltpu.VMEM(arrived.shape if count else (PIECES, 8, PB), jnp.float32),
            product_scratch(vectors),
            pltpu.SemaphoreType.DMA((PIECES,)),
            pltpu.SemaphoreType.DMA,
        ],
        compiler_params=params(24),
        name="finish",
    )(where, places, arrived, total, *vectors)


def swap(x, axis, mask):
    return lax.ppermute(x, axis, [(i, i ^ mask) for i in range(lax.axis_size(axis))])


def gather_columns(own):
    half = lax.axis_size("col") // 2
    far = swap(own, "col", half)
    near = [own] + [swap(own, "col", mask) for mask in range(1, half)]
    beyond = [far] + [swap(far, "col", mask) for mask in range(1, half)]
    return near, beyond


def sum_rows(keep, away):
    mask = 1
    while True:
        summed = keep + swap(away, "row", mask)
        mask *= 2
        if mask == lax.axis_size("row"):
            return summed[0]
        keep, away = summed[0::2], summed[1::2]


def exchange(x):
    return lax.all_to_all(x, BOTH, split_axis=0, concat_axis=0, tiled=True)


def body(resid_deriv, local_deriv, inv_factor, block_ids, right_sides, damping):
    n_row, n_col = lax.axis_size("row"), lax.axis_size("col")
    devices = n_row * n_col
    capacity = max(block_ids.shape[1] // n_row, 1)
    chunks = chunk_list(capacity)
    row_index, col_index = lax.axis_index("row"), lax.axis_index("col")
    where = jnp.stack([col_index * n_row + row_index, row_index, col_index]).astype(jnp.int32)

    sends = region(
        block_ids, resid_deriv, local_deriv, inv_factor, n_row, n_col, capacity, chunks
    )
    arrived = []
    for x in sends:
        arrived.append(exchange(x))
    places = arrived[0][:, PB : PB + capacity, 0].astype(jnp.int32)

    total, pivot = first_tiles(where, places, arrived[0], damping[None, :], devices)
    factor = lax.linalg.cholesky(pivot, symmetrize_input=False)
    inverse, residual, update = invert(factor, right_sides)
    close, beyond = gather_columns(update)

    for (slot, first, count), x in list(zip(chunks, arrived))[1:-1]:
        total = more_tiles(places, x, total, slot, first, count)
    slot, first, count = chunks[-1]
    high, low, near, total = finish(
        where, places, arrived[-1], total, close, n_row, slot, first, count if slot else 0
    )
    high_dot = functools.partial(jnp.dot, precision=lax.Precision.HIGHEST)
    keep, away = far_product(where, near, high, low, beyond)
    answer = update
    weight = 1.0 / ratio
    for sweep in range(1, ITERS):
        residual = residual - sum_rows(keep, away)
        weight_next = 1.0 / (2.0 * ratio - weight)
        update = weight_next * weight * update + 2.0 * weight_next / radius * high_dot(
            residual, inverse
        )
        weight = weight_next
        answer = answer + update
        if sweep + 1 < ITERS:
            close, beyond = gather_columns(update)
            near, normal = near_product(where, high, low, total, close)
            keep, away = far_product(where, near, high, low, beyond)
    return normal, answer.T


def solution(mesh):
    return jax.shard_map(
        body,
        mesh=mesh,
        in_specs=(
            P(BOTH, None, None),
            P(BOTH, None, None),
            P(BOTH, None, None),
            P(BOTH, None),
            P(("col", "row"), None),
            P(("col", "row")),
        ),
        out_specs=(P(None, "row", None, "col"), P(("col", "row"), None)),
        check_vma=False,
    )
```

```python
import functools

import jax
import jax.numpy as jnp
from jax import lax
from jax.experimental import pallas as pl
from jax.experimental.pallas import tpu as pltpu
from jax.sharding import PartitionSpec as P


PB = 128
ITERS = 3
AHEAD = 2
PIECES = 4

cheb_low = 0.05
cheb_high = 2.0
center = (cheb_high + cheb_low) / 2.0
radius = (cheb_high - cheb_low) / 2.0
ratio = center / radius

BOTH = ("row", "col")
VMEM = pl.BlockSpec(memory_space=pltpu.VMEM)
SMEM = pl.BlockSpec(memory_space=pltpu.SMEM)
ANY = pl.BlockSpec(memory_space=pl.ANY)
HBM = pl.BlockSpec(memory_space=pltpu.HBM)
f32_dot = functools.partial(jnp.dot, preferred_element_type=jnp.float32)


def params(mib):
    return pltpu.CompilerParams(vmem_limit_bytes=mib << 20)


def split(x):
    high = x.astype(jnp.bfloat16)
    return high, (x - high.astype(jnp.float32)).astype(jnp.bfloat16)


def dot_split(a, b):
    (ah, al), (bh, bl) = a, b
    return f32_dot(ah, bh) + (f32_dot(ah, bl) + f32_dot(al, bh))


def chunk_list(capacity):
    chunks = [(0, 0, PB + 8)]
    for slot in range(1, capacity):
        chunks.append((slot, 0, PB))
    return chunks


def region_kernel(n_row, n_col, capacity, chunks, ids_in, resid, local_in, factor_in, *refs):
    outs = refs[: len(chunks)]
    bundles, _, gp = resid.shape
    blocks, n = gp // PB, factor_in.shape[2]
    refs = refs[len(chunks) :]
    cols, rows, coupled = refs[:bundles], refs[bundles : 2 * bundles], refs[2 * bundles :][:2]
    ids, raw, partial, down, across, local, factor, stage, sector, in_sem, small_sem, out_sem = refs[
        2 * bundles + 2 :
    ]

    fetch_ids = pltpu.make_async_copy(ids_in, ids, small_sem.at[0])
    fetch_local = pltpu.make_async_copy(local_in, local, small_sem.at[1])
    fetch_factor = pltpu.make_async_copy(factor_in, factor, small_sem.at[2])
    fetches = [
        pltpu.make_async_copy(resid.at[b], raw.at[b], in_sem.at[b]) for b in range(bundles)
    ]
    ahead = min(AHEAD, bundles)
    fetch_ids.start()
    for fetch in fetches[:ahead]:
        fetch.start()
    fetch_local.start()
    stage[0, :, PB:, :] = jnp.full((n_row * n_col, 8, PB), -1.0, jnp.float32)
    fetch_ids.wait()

    def arrange(b):
        fetches[b].wait()
        if b == 0:
            fetch_factor.start()
        if b + ahead < bundles:
            fetches[b + ahead].start()
        for k in range(blocks):
            rank = jnp.int32(0)
            for j in range(blocks):
                if j != k:
                    rank = rank + (ids[b, j] < ids[b, k]).astype(jnp.int32)
            if b == 0:
                sector[rank] = ids[b, k]
            block = raw[b, :, k * PB : (k + 1) * PB]
            cols[b][rank] = block
            rows[b][pl.ds(pl.multiple_of(rank * PB, PB), PB), :] = block.T

    def couple(b):
        if b == 0:
            fetch_local.wait()
        coupled[b % 2][...] = f32_dot(rows[b][...], local[b])

    def project(b):
        if b == 0:
            fetch_factor.wait()
        ch, cl = split(coupled[b % 2][...])
        fh, fl = split(factor[b])
        terms = jnp.concatenate([fh, fl], axis=1)
        parts = f32_dot(jnp.concatenate([ch, cl], axis=1), jnp.concatenate([terms, terms], axis=0))
        projected = (parts[:, :n] + parts[:, n:]).astype(jnp.bfloat16)
        across[:, b * n : (b + 1) * n] = -projected
        for p in range(blocks):
            down[p, b * n : (b + 1) * n, :] = projected[p * PB : (p + 1) * PB].T

    def gram(i, j, picked, last):
        left = [rows[b][i * PB : (i + 2) * PB, :] for b in picked]
        pair = [[cols[b][j + x] for b in picked] for x in range(2)]
        if last:
            left.append(across[i * PB : (i + 2) * PB, :])
            pair = [parts + [down[j + x]] for x, parts in enumerate(pair)]
        right = jnp.concatenate([jnp.concatenate(parts, axis=0) for parts in pair], axis=1)
        return f32_dot(jnp.concatenate(left, axis=1), right)

    pairs = [(i, j) for i in range(0, blocks, 2) for j in range(i, blocks, 2)]
    middle = bundles // 2
    steps = bundles + 2
    early = steps - middle
    for step in range(steps):
        if step >= middle:
            for at in range((step - middle) * len(pairs) // early, (step - middle + 1) * len(pairs) // early):
                partial[at] = gram(*pairs[at], range(middle), False)
        if step < bundles:
            arrange(step)
        if 1 <= step <= bundles:
            couple(step - 1)
        if step >= 2:
            project(step - 2)

    def target(g, h):
        mine, other = sector[g], sector[h]
        residue = lax.rem(mine, n_row)
        slot = jnp.int32(0)
        if g != h:
            for j in range(g):
                slot = slot + (lax.rem(sector[j], n_row) == residue).astype(jnp.int32)
        if g < h:
            slot = slot + (lax.rem(other, n_row) == residue).astype(jnp.int32)
        place = mine - residue + lax.rem(other, n_row)
        return slot, residue * n_col + lax.div(other, n_row), place

    def put(g, h, tile):
        slot, owner, place = target(g, h)
        stage[slot, owner, :PB, :] = tile
        stage[0, owner, pl.ds(PB + slot, 1), :] = jnp.full((1, PB), place.astype(jnp.float32))

    def send(g, h):
        slot, owner, _ = target(g, h)
        tile = stage.at[slot, owner, pl.ds(0, PB), :]
        for out, (at_slot, _, _) in zip(outs, chunks):

            @pl.when(slot == at_slot)
            def _():
                there = out.at[owner, pl.ds(0, PB), :]
                pltpu.make_async_copy(tile, there, out_sem.at[0]).start()

    for at, (i, j) in enumerate(pairs):
        total = partial[at] + gram(i, j, range(middle, bundles), True)
        for x in range(2):
            for y in range(2):
                tile = total[x * PB : (x + 1) * PB, y * PB : (y + 1) * PB]
                put(i + x, j + y, tile)
                if i != j:
                    put(j + y, i + x, tile.T)
        if j + 2 == blocks:
            for x in range(2):
                for h in range(blocks):
                    send(i + x, h)
    marks = pltpu.make_async_copy(
        stage.at[0, :, pl.ds(PB, 8), :], outs[0].at[:, pl.ds(PB, 8), :], out_sem.at[1]
    )
    marks.start()
    marks.wait()
    sent = stage.at[:, pl.ds(0, blocks * blocks // capacity), pl.ds(0, PB), :]
    pltpu.make_async_copy(sent, sent, out_sem.at[0]).wait()


def region(ids, resid, local, factor, n_row, n_col, capacity, chunks):
    bundles, m, gp = resid.shape
    blocks, n = ids.shape[1], local.shape[2]
    return pl.pallas_call(
        functools.partial(region_kernel, n_row, n_col, capacity, chunks),
        out_shape=[
            jax.ShapeDtypeStruct((n_row * n_col, count, PB), jnp.float32) for _, _, count in chunks
        ],
        in_specs=[HBM] * 4,
        out_specs=[HBM] * len(chunks),
        scratch_shapes=[pltpu.VMEM((blocks, m, PB), jnp.bfloat16)] * bundles
        + [pltpu.VMEM((gp, m), jnp.bfloat16)] * bundles
        + [pltpu.VMEM((gp, n), jnp.float32)] * 2
        + [
            pltpu.SMEM(ids.shape, jnp.int32),
            pltpu.VMEM(resid.shape, resid.dtype),
            pltpu.VMEM((blocks * (blocks + 2) // 8, 2 * PB, 2 * PB), jnp.float32),
            pltpu.VMEM((blocks, bundles * n, PB), jnp.bfloat16),
            pltpu.VMEM((gp, bundles * n), jnp.bfloat16),
            pltpu.VMEM(local.shape, local.dtype),
            pltpu.VMEM(factor.shape, factor.dtype),
            pltpu.VMEM((capacity, n_row * n_col, PB + 8, PB), jnp.float32),
            pltpu.SMEM((blocks,), jnp.int32),
            pltpu.SemaphoreType.DMA((bundles,)),
            pltpu.SemaphoreType.DMA((3,)),
            pltpu.SemaphoreType.DMA((2,)),
        ],
        compiler_params=params(63),
        name="region",
    )(ids, resid, local, factor)


def add_tiles(places, slot, arrived, total, first, count, start=0, size=None):
    def step(d, carry):
        place = places[d, slot]

        @pl.when(place >= 0)
        def _():
            total[place, pl.ds(first, count), :] += arrived[d, :count, :]

        return carry

    lax.fori_loop(start, start + (size or arrived.shape[0]), step, 0)


def first_kernel(where, places, arrived, damping, total, pivot, held, sem):
    fetch = pltpu.make_async_copy(arrived, held, sem)
    fetch.start()
    total[...] = jnp.zeros_like(total)
    fetch.wait()
    add_tiles(places, 0, held, total, 0, PB)
    line = lax.broadcasted_iota(jnp.int32, (PB, PB), 0)
    column = lax.broadcasted_iota(jnp.int32, (PB, PB), 1)
    corner = total[where[0]] + jnp.where(line == column, damping[...], 0.0)
    total[where[0]] = corner
    pivot[...] = corner


def first_tiles(where, places, arrived, damping, tiles):
    return pl.pallas_call(
        first_kernel,
        out_shape=[
            jax.ShapeDtypeStruct((tiles, PB, PB), jnp.float32),
            jax.ShapeDtypeStruct((PB, PB), jnp.float32),
        ],
        in_specs=[SMEM, SMEM, ANY, VMEM],
        out_specs=[VMEM, VMEM],
        scratch_shapes=[pltpu.VMEM(arrived.shape, jnp.float32), pltpu.SemaphoreType.DMA],
        compiler_params=params(24),
        name="first_tiles",
    )(where, places, arrived, damping)


def invert_kernel(factor, rhs, inverse, turned, update):
    line = lax.broadcasted_iota(jnp.int32, (PB, PB), 0)
    column = lax.broadcasted_iota(jnp.int32, (PB, PB), 1)

    def product(a, b):
        return dot_split(split(a), split(b))

    c = jnp.where(line >= column, factor[...], 0.0)
    diagonal = jnp.sum(jnp.where(line == column, c, 0.0), axis=1, keepdims=True)
    scale = 1.0 / diagonal
    unit = c * scale
    eye = jnp.where(line == column, 1.0, 0.0)
    size = 4
    near = jnp.where((line // size == column // size) & (line > column), unit, 0.0)
    second = product(near, near)
    grown = (eye - near) + product(eye - near, second)
    while size < PB:
        size *= 2
        link = jnp.where(
            (line // size == column // size) & (line // (size // 2) != column // (size // 2)), unit, 0.0
        )
        grown = grown - product(product(grown, link), grown)
    across = jnp.sum(jnp.where(line == column, c, 0.0), axis=0, keepdims=True)
    lower = grown * (1.0 / across)
    full = product(lower.T, lower)
    inverse[...] = full
    back = rhs[...].T
    turned[...] = back
    update[...] = product(back, full) / center


def invert(factor, rhs):
    wide = rhs.shape[1]
    return pl.pallas_call(
        invert_kernel,
        out_shape=[
            jax.ShapeDtypeStruct((PB, PB), jnp.float32),
            jax.ShapeDtypeStruct((wide, PB), jnp.float32),
            jax.ShapeDtypeStruct((wide, PB), jnp.float32),
        ],
        in_specs=[VMEM, VMEM],
        out_specs=[VMEM] * 3,
        compiler_params=params(8),
        name="invert",
    )(factor, rhs)


def more_kernel(slot, first, count, places, arrived, total_in, total, held, sem):
    fetch = pltpu.make_async_copy(arrived, held, sem)
    fetch.start()
    fetch.wait()
    add_tiles(places, slot, held, total, first, count)


def more_tiles(places, arrived, total, slot, first, count):
    return pl.pallas_call(
        functools.partial(more_kernel, slot, first, count),
        out_shape=jax.ShapeDtypeStruct(total.shape, jnp.float32),
        in_specs=[SMEM, ANY, VMEM],
        out_specs=VMEM,
        input_output_aliases={2: 0},
        scratch_shapes=[pltpu.VMEM(arrived.shape, jnp.float32), pltpu.SemaphoreType.DMA],
        compiler_params=params(12),
        name="more_tiles",
    )(places, arrived, total)


def half_product(where, side, vectors, high, low, both):
    half = len(vectors)
    for mask, vector in enumerate(vectors):
        at = pl.multiple_of((lax.rem(where[2], half) ^ mask) * PB, PB)
        vh, vl = split(vector[...])
        both[0, :, pl.ds(at, PB)] = vh
        both[1, :, pl.ds(at, PB)] = vl
    rows = pl.ds(pl.multiple_of((lax.div(where[2], half) ^ side) * (half * PB), half * PB), half * PB)
    return dot_split((both[0], both[1]), (high[rows, :], low[rows, :]))


def plain_kernel(half, where, high, low, *refs):
    vectors, (near, both) = refs[:half], refs[half:]
    near[...] = half_product(where, 0, vectors, high, low, both)


def near_kernel(half, where, high, low, total, *refs):
    vectors, (near, normal, both, whole, sem) = refs[:half], refs[half:]
    n_col, n_row = whole.shape[0], whole.shape[2] // PB
    stores = []
    for a in range(n_col):
        for sub in range(n_row):
            whole[a, :, sub * PB : (sub + 1) * PB] = total[a * n_row + sub]
        stores.append(pltpu.make_async_copy(whole.at[a], normal.at[a, 0], sem.at[a]))
        stores[-1].start()
    near[...] = half_product(where, 0, vectors, high, low, both)
    for store in stores:
        store.wait()


def far_kernel(half, where, near, high, low, *refs):
    vectors, (keep, away, both) = refs[:half], refs[half:]
    result = near[...] + half_product(where, 1, vectors, high, low, both)
    odd = lax.rem(where[1], 2) == 1
    for i in range(keep.shape[0]):
        one = result[:, 2 * i * PB : (2 * i + 1) * PB]
        two = result[:, (2 * i + 1) * PB : (2 * i + 2) * PB]
        at = lax.div(where[1], 2) ^ i
        keep[at] = jnp.where(odd, two, one)
        away[at] = jnp.where(odd, one, two)


def product_scratch(vectors):
    return pltpu.VMEM((2, vectors[0].shape[0], len(vectors) * PB), jnp.bfloat16)


def near_product(where, high, low, total, vectors):
    n_col, n_row = high.shape[0] // PB, high.shape[1] // PB
    if total is None:
        near = pl.pallas_call(
            functools.partial(plain_kernel, len(vectors)),
            out_shape=jax.ShapeDtypeStruct((vectors[0].shape[0], high.shape[1]), jnp.float32),
            in_specs=[SMEM, VMEM, VMEM] + [VMEM] * len(vectors),
            out_specs=VMEM,
            scratch_shapes=[product_scratch(vectors)],
            compiler_params=params(12),
            name="first_product",
        )(where, high, low, *vectors)
        return near, None
    return pl.pallas_call(
        functools.partial(near_kernel, len(vectors)),
        out_shape=[
            jax.ShapeDtypeStruct((vectors[0].shape[0], high.shape[1]), jnp.float32),
            jax.ShapeDtypeStruct((n_col, 1, PB, n_row * PB), jnp.float32),
        ],
        in_specs=[SMEM, VMEM, VMEM, VMEM] + [VMEM] * len(vectors),
        out_specs=[VMEM, ANY],
        scratch_shapes=[
            product_scratch(vectors),
            pltpu.VMEM((n_col, PB, n_row * PB), jnp.float32),
            pltpu.SemaphoreType.DMA((n_col,)),
        ],
        compiler_params=params(16),
        name="near_product",
    )(where, high, low, total, *vectors)


def far_product(where, near, high, low, vectors):
    n_row = high.shape[1] // PB
    halves = jax.ShapeDtypeStruct((n_row // 2, vectors[0].shape[0], PB), jnp.float32)
    return pl.pallas_call(
        functools.partial(far_kernel, len(vectors)),
        out_shape=[halves, halves],
        in_specs=[SMEM, VMEM, VMEM, VMEM] + [VMEM] * len(vectors),
        out_specs=[VMEM] * 2,
        scratch_shapes=[product_scratch(vectors)],
        compiler_params=params(12),
        name="far_product",
    )(where, near, high, low, *vectors)


def finish_kernel(slot, first, count, places, arrived, total_in, *refs):
    high, low, total, held, in_sem, total_sem = refs
    n_col, n_row = high.shape[0] // PB, high.shape[1] // PB
    bring = pltpu.make_async_copy(total_in, total, total_sem)
    bring.start()
    pieces = PIECES if count else 0
    size = held.shape[0] // PIECES
    fetches = [
        pltpu.make_async_copy(
            arrived.at[pl.ds(p * size, size)], held.at[pl.ds(p * size, size)], in_sem.at[p]
        )
        for p in range(pieces)
    ]
    for fetch in fetches:
        fetch.start()
    bring.wait()
    for p, fetch in enumerate(fetches):
        fetch.wait()
        add_tiles(places, slot, held, total, first, count, p * size, size)
    for a in range(n_col):
        for sub in range(n_row):
            th, tl = split(total[a * n_row + sub])
            high[a * PB : (a + 1) * PB, sub * PB : (sub + 1) * PB] = th
            low[a * PB : (a + 1) * PB, sub * PB : (sub + 1) * PB] = tl


def finish(places, arrived, total, n_row, n_col, slot, first, count):
    split_matrix = jax.ShapeDtypeStruct((n_col * PB, n_row * PB), jnp.bfloat16)
    return pl.pallas_call(
        functools.partial(finish_kernel, slot, first, count),
        out_shape=[
            split_matrix,
            split_matrix,
            jax.ShapeDtypeStruct(total.shape, jnp.float32),
        ],
        in_specs=[SMEM, ANY, ANY],
        out_specs=[VMEM] * 3,
        scratch_shapes=[
            pltpu.VMEM(arrived.shape if count else (PIECES, 8, PB), jnp.float32),
            pltpu.SemaphoreType.DMA((PIECES,)),
            pltpu.SemaphoreType.DMA,
        ],
        compiler_params=params(24),
        name="finish",
    )(places, arrived, total)


def swap(x, axis, mask):
    return lax.ppermute(x, axis, [(i, i ^ mask) for i in range(lax.axis_size(axis))])


def gather_columns(own):
    half = lax.axis_size("col") // 2
    far = swap(own, "col", half)
    near = [own] + [swap(own, "col", mask) for mask in range(1, half)]
    beyond = [far] + [swap(far, "col", mask) for mask in range(1, half)]
    return near, beyond


def sum_rows(keep, away):
    mask = 1
    while True:
        summed = keep + swap(away, "row", mask)
        mask *= 2
        if mask == lax.axis_size("row"):
            return summed[0]
        keep, away = summed[0::2], summed[1::2]


def exchange(x):
    return lax.all_to_all(x, BOTH, split_axis=0, concat_axis=0, tiled=True)


def body(resid_deriv, local_deriv, inv_factor, block_ids, right_sides, damping):
    n_row, n_col = lax.axis_size("row"), lax.axis_size("col")
    devices = n_row * n_col
    capacity = max(block_ids.shape[1] // n_row, 1)
    chunks = chunk_list(capacity)
    row_index, col_index = lax.axis_index("row"), lax.axis_index("col")
    where = jnp.stack([col_index * n_row + row_index, row_index, col_index]).astype(jnp.int32)

    sends = region(
        block_ids, resid_deriv, local_deriv, inv_factor, n_row, n_col, capacity, chunks
    )
    arrived = []
    for x in sends:
        arrived.append(exchange(x))
    places = arrived[0][:, PB : PB + capacity, 0].astype(jnp.int32)

    total, pivot = first_tiles(where, places, arrived[0], damping[None, :], devices)
    factor = lax.linalg.cholesky(pivot, symmetrize_input=False)
    inverse, residual, update = invert(factor, right_sides)
    close, beyond = gather_columns(update)

    for (slot, first, count), x in list(zip(chunks, arrived))[1:-1]:
        total = more_tiles(places, x, total, slot, first, count)
    slot, first, count = chunks[-1]
    high, low, total = finish(
        places, arrived[-1], total, n_row, n_col, slot, first, count if slot else 0
    )
    near, _ = near_product(where, high, low, None, close)
    high_dot = functools.partial(jnp.dot, precision=lax.Precision.HIGHEST)
    keep, away = far_product(where, near, high, low, beyond)
    answer = update
    weight = 1.0 / ratio
    for sweep in range(1, ITERS):
        residual = residual - sum_rows(keep, away)
        weight_next = 1.0 / (2.0 * ratio - weight)
        update = weight_next * weight * update + 2.0 * weight_next / radius * high_dot(
            residual, inverse
        )
        weight = weight_next
        answer = answer + update
        if sweep + 1 < ITERS:
            close, beyond = gather_columns(update)
            near, normal = near_product(where, high, low, total, close)
            keep, away = far_product(where, near, high, low, beyond)
    return normal, answer.T


def solution(mesh):
    return jax.shard_map(
        body,
        mesh=mesh,
        in_specs=(
            P(BOTH, None, None),
            P(BOTH, None, None),
            P(BOTH, None, None),
            P(BOTH, None),
            P(("col", "row"), None),
            P(("col", "row")),
        ),
        out_specs=(P(None, "row", None, "col"), P(("col", "row"), None)),
        check_vma=False,
    )
```
